512 devices in a mesh: ctx: 64 (over y, z_lo, core), exp: 8 (over z_hi, x).
Axes of the slice: x: 4, y: 4, z: 16 (z_hi: 2, z_lo: 8; z = z_hi * 8 + z_lo), core: 2. Of those that a mesh axis runs over, the one named last changes fastest.
Arguments:
- queries: bfloat16 [8192, 32, 128], P('ctx', 'exp'), may hold values from -100 to 100
- keys: bfloat16 [8192, 2, 128], P('ctx'), may hold values from -4 to 4
- values: bfloat16 [8192, 2, 128], P('ctx'), may hold values from -4 to 4
- resid: bfloat16 [8192, 4096], P('ctx', 'exp'), may hold values from -20 to 20
- gain: float32 [4096], P('exp'), may hold values from 0.1 to 1.9
- expert_ids: int32 [8192, 8], P('ctx'), may hold values from 0 to 127, all different within a row; in each aligned block of 128 rows (0 to 127, 128 to 255, ...) at most 10 rows name the same one
- gate_scores: float32 [8192, 8], P('ctx'), may hold values from 0.05 to 1
- w_gate_up: bfloat16 [64, 4096, 2, 768], P('ctx', 'exp'), may hold values from -0.09375 to 0.09375
- w_down: bfloat16 [64, 768, 4096], P('ctx', None, 'exp'), may hold values from -0.625 to 0.625
- w_out: bfloat16 [32, 128, 4096], P('exp', 'ctx'), may hold values from -0.5 to 0.5
Outputs:
- context: bfloat16 [8192, 32, 128], P('ctx', 'exp')
- mixed: bfloat16 [8192, 4096], P('ctx', 'exp')
The draws below stay inside these ranges and needn't reach their ends.
Inputs may be any that keep to these rules, and one draw needn't show every extreme that they name: `expert_ids`: each row names 8 different experts; within the 128 rows of one index of ctx no expert is named more than 10 times.
All inputs are finite; a program needn't handle non-finite values.
Results may differ from the reference program's by a relative error of at most 0.02.
Values may be sent and summed in bfloat16 or wider, within the bound.
No kernel may reach another device: no remote copies, remote signals or barrier semaphores. Data moves between devices by JAX's collectives and lax.ppermute only.
A program may use at most 64 MiB of HBM per device.

```python
import math
import jax
import jax.numpy as jnp
import numpy as np
from jax import lax

D = 4096
HQ = 32
KVH = 2
HD = 128
FF = 768
EXPERTS = 128
TOPK = 8
T_DEV = 128
SEQ = 8192
MOST = 10
FLIGHT = 64
N_CTX = 64
N_EXP = 8


def final_keys(key):
    keys_base = jnp.clip(jax.random.normal(jax.random.fold_in(key, 101), (SEQ, KVH, HD), jnp.float32), -4.0, 4.0)
    return keys_base


def draw_keys(key, part):
    return final_keys(key).astype(jnp.bfloat16)


def draw_queries(key, part):
    raw_draw = jnp.clip(jax.random.normal(jax.random.fold_in(key, 301), (SEQ, HQ, HD), jnp.float32), -4.0, 4.0)
    return raw_draw.astype(jnp.bfloat16)


def draw_resid(key, part):
    normal_part = jnp.clip(jax.random.normal(jax.random.fold_in(key, 401), (SEQ, D), jnp.float32), -4.0, 4.0)
    row_scale = jnp.exp(jax.random.uniform(jax.random.fold_in(key, 402), (SEQ, 1), jnp.float32, math.log(0.3), math.log(3.0)))
    column_rough = jnp.exp(jax.random.uniform(jax.random.fold_in(key, 403), (1, D), jnp.float32, math.log(0.5), math.log(2.0)))
    fraction = jnp.arange(D).astype(jnp.float32)[None, :] / (D - 1) - 0.5
    rising = jnp.exp(math.log(3.0) * fraction)
    drawn_value = jnp.clip(0.4 * normal_part * row_scale * column_rough * rising, -20.0, 20.0)
    return drawn_value.astype(jnp.bfloat16)


def level_of(key, dims, cuts, low, top_value):
    def one(dim, parts):
        heights = jax.random.uniform(jax.random.fold_in(jax.random.fold_in(key, 6), dim), (parts,), jnp.float32, low / len(cuts), top_value / len(cuts))
        return jnp.repeat(jnp.exp(heights), dims[dim] // parts).reshape((-1,) + (1,) * (len(dims) - dim - 1))

    level = one(*cuts[0])
    for cut in cuts[1:]:
        level = level * one(*cut)
    return level


def deal_out(rng, own, number, rows, count, top, bound, lean):
    ranking = jax.random.permutation(rng, count)
    crowded, ordinary = load_shares(count, rows * top, bound, lean, True), load_shares(count, rows * top, bound, lean, False)
    places = jnp.arange(count)

    def named(tallies, turn):
        used = int((tallies > 0).sum())
        fixed = max(1, used // 4)
        passed = fixed + (places - fixed + turn * (used - fixed)) % max(1, count - fixed)
        return jnp.zeros((count,), jnp.int32).at[ranking[jnp.where(places < fixed, places, passed)]].set(jnp.asarray(tallies, jnp.int32))

    tallies = jnp.where(number % 4 == 0, named(crowded, number // 4), named(ordinary, number - number // 4 - 1))
    mixed = jax.random.permutation(jax.random.fold_in(own, 3), count)
    giver, sink = mixed[0:count // 2 * 2:2], mixed[1:count // 2 * 2:2]
    slack = jnp.minimum(tallies[giver] - 1, bound - tallies[sink]) // 2
    slack = jnp.where((giver == ranking[0]) | (sink == ranking[0]) | (tallies[sink] == 0), 0, jnp.maximum(slack, 0))
    passed = jax.random.randint(jax.random.fold_in(own, 4), (count // 2,), 0, 1 << 20) % (slack + 1)
    tallies = tallies.at[giver].add(-passed).at[sink].add(passed)
    labels = jnp.searchsorted(jnp.cumsum(tallies), jnp.arange(rows * top), side="right").astype(jnp.int32)
    table = labels.reshape(top, rows).T
    table = table[jax.random.permutation(jax.random.fold_in(own, 1), rows)]
    turn = jax.random.randint(jax.random.fold_in(own, 2), (rows, 1), 0, top)
    return jnp.take_along_axis(table, (jnp.arange(top)[None, :] + turn) % top, axis=1)


def load_shares(count, total, reach, lean, full):
    weights = [(1 << 20) // math.isqrt(standing ** lean) + 1 for standing in range(1, count + 1)]
    largest = reach if full else min(reach, max(-(-total // count), total * weights[0] // sum(weights)))
    least = 1 if total - largest >= count - 1 else 0
    given, rest = [largest] + [least] * (count - 1), total - largest - least * (count - 1)
    while rest > 0:
        candidates = [i for i in range(1, count) if given[i] < largest] or [i for i in range(1, count) if given[i] < reach]
        pool, left = sum([weights[i] for i in candidates]), rest
        for i in candidates:
            more = min(reach - given[i], max(1, left * weights[i] // pool), rest)
            given[i] = given[i] + more
            rest = rest - more
    return np.array(given)


def bell_draw(own_key, shape, spread, limit, pieces=(), held_as=jnp.bfloat16):
    level = level_of(own_key, shape, pieces, -0.22, 0.18) if pieces else 1.0
    values = jax.random.normal(own_key, shape, jnp.float32) * spread * level
    return jnp.minimum(jnp.maximum(values, -limit), limit).astype(held_as)


def setup_inputs(seed: int = 0) -> dict:
    key_list = jax.random.split(jax.random.key(seed), 11)
    queries = draw_queries(jax.random.fold_in(key_list[10], 71), 0)
    keys = draw_keys(jax.random.fold_in(key_list[10], 71), 0)
    values = bell_draw(key_list[2], (SEQ, KVH, HD), 1.0, 4.0, ((0, 64),))
    resid = draw_resid(jax.random.fold_in(key_list[10], 71), 0)
    gain = jnp.clip(1.0 + 0.18 * jax.random.normal(key_list[4], (D,), jnp.float32), 0.1, 1.9)
    expert_ids_keys = jax.random.split(jax.random.fold_in(key_list[5], 1), SEQ // T_DEV)
    expert_ids_turns = jax.random.permutation(jax.random.fold_in(key_list[5], 3), SEQ // T_DEV)
    expert_ids = jax.vmap(lambda own, number: deal_out(jax.random.fold_in(key_list[5], 2), own, number, T_DEV, EXPERTS, TOPK, MOST, 2))(expert_ids_keys, expert_ids_turns).reshape((SEQ, TOPK))
    gate_scores = jnp.clip(0.05 + 0.95 * jax.random.uniform(key_list[6], (SEQ, TOPK), jnp.float32) ** level_of(key_list[6], (SEQ, TOPK), ((0, 64),), -0.2, 0.2), 0.05, 1.0)
    w_gate_up = bell_draw(key_list[7], (FLIGHT, D, 2, FF), D ** -0.5, 0.09375, ((0, 64), (1, 8)))
    w_down = bell_draw(key_list[8], (FLIGHT, FF, D), (FF // 8) ** -0.5, 0.625, ((0, 64), (2, 8)))
    w_out = bell_draw(key_list[9], (HQ, HD, D), HD ** -0.5, 0.5, ((0, 8), (1, 64)))
    return {"queries": queries, "keys": keys, "values": values, "resid": resid, "gain": gain, "expert_ids": expert_ids, "gate_scores": gate_scores, "w_gate_up": w_gate_up, "w_down": w_down, "w_out": w_out}


def keep_round(value):
    rounded = value.astype(jnp.bfloat16)
    return lax.optimization_barrier(rounded).astype(jnp.float32)

def reference(queries, keys, values, resid, gain, expert_ids, gate_scores, w_gate_up, w_down, w_out):
    group_size = HQ // KVH
    head_group = (jnp.arange(HQ) // group_size).astype(jnp.int32)
    keys_wide = jnp.take(keys, head_group, axis=1).astype(jnp.float32)
    values_wide = jnp.take(values, head_group, axis=1).astype(jnp.float32)
    scaling = 1.0 / math.sqrt(HD)
    positions = jnp.arange(SEQ).astype(jnp.int32)

    def attend(block_index):
        start_row = (block_index * T_DEV).astype(jnp.int32)
        query_block = lax.dynamic_slice_in_dim(queries, start_row, T_DEV, 0).astype(jnp.float32)
        scores = jnp.einsum('thd,shd->hts', query_block, keys_wide) * scaling
        query_pos = start_row + jnp.arange(T_DEV).astype(jnp.int32)
        visible = positions[None, None, :] <= query_pos[None, :, None]
        masked = jnp.where(visible, scores, -1e+30)
        highest = lax.optimization_barrier(jnp.max(masked, axis=2, keepdims=True))
        weights_exp = jnp.where(visible, jnp.exp(masked - highest), 0.0)
        denominator = lax.optimization_barrier(jnp.sum(weights_exp, axis=2))
        numerator = jnp.einsum('hts,shd->thd', keep_round(weights_exp), values_wide)
        return (numerator / jnp.transpose(denominator)[:, :, None]).astype(jnp.bfloat16)
    context = lax.map(attend, jnp.arange(N_CTX).astype(jnp.int32)).reshape(SEQ, HQ, HD)
    heads_local = HQ // N_EXP
    weight_groups = w_out.astype(jnp.float32).reshape(N_EXP, heads_local * HD, D)

    def project(block_index):
        start_row = (block_index * T_DEV).astype(jnp.int32)
        context_block = lax.dynamic_slice_in_dim(context, start_row, T_DEV, 0).astype(jnp.float32)
        context_block = context_block.reshape(T_DEV, N_EXP, heads_local * HD)
        partial_sum = jnp.einsum('teh,ehd->ted', context_block, weight_groups)
        return lax.optimization_barrier(jnp.sum(keep_round(partial_sum), axis=1))
    attended = lax.map(project, jnp.arange(N_CTX).astype(jnp.int32)).reshape(SEQ, D)
    hidden_state = resid.astype(jnp.float32) + attended
    mean_square = lax.optimization_barrier(jnp.mean(hidden_state * hidden_state, axis=1, keepdims=True))
    normed = (hidden_state * lax.rsqrt(mean_square + 1e-06) * gain[None, :]).astype(jnp.bfloat16)
    per_block = expert_ids.reshape(N_CTX, T_DEV * TOPK).astype(jnp.int32)
    onehot = (per_block[:, :, None] == jnp.arange(FLIGHT).astype(jnp.int32)[None, None, :]).astype(jnp.int32)
    earlier = jnp.cumsum(onehot, axis=1) - onehot
    rank_of = lax.optimization_barrier(jnp.sum(earlier * onehot, axis=2)).astype(jnp.int32)
    active = per_block < FLIGHT
    slot_of = jnp.where(active, per_block * MOST + rank_of, FLIGHT * MOST).astype(jnp.int32)
    token_global = (jnp.arange(N_CTX)[:, None] * T_DEV + jnp.arange(T_DEV * TOPK)[None, :] // TOPK).astype(jnp.int32)
    mixing = (gate_scores / lax.optimization_barrier(jnp.sum(gate_scores, axis=1, keepdims=True))).reshape(N_CTX, T_DEV * TOPK)
    source_index = jnp.broadcast_to(jnp.arange(N_CTX).astype(jnp.int32)[:, None], per_block.shape)
    slot_token = jnp.zeros((N_CTX, FLIGHT * MOST), jnp.int32).at[source_index, slot_of].set(token_global, mode='drop')
    slot_weight = jnp.zeros((N_CTX, FLIGHT * MOST), jnp.float32).at[source_index, slot_of].set(mixing, mode='drop')
    slot_active = jnp.zeros((N_CTX, FLIGHT * MOST), jnp.float32).at[source_index, slot_of].set(1.0, mode='drop')

    def one_expert(moe_sum, expert_index):
        begin = (expert_index * MOST).astype(jnp.int32)
        tokens_for = lax.dynamic_slice_in_dim(slot_token, begin, MOST, 1).reshape(-1)
        weights_for = lax.dynamic_slice_in_dim(slot_weight, begin, MOST, 1).reshape(-1)
        active_for = lax.dynamic_slice_in_dim(slot_active, begin, MOST, 1).reshape(-1)
        row_block = jnp.take(normed, tokens_for, axis=0) * active_for[:, None].astype(jnp.bfloat16)
        weights_gu = lax.dynamic_index_in_dim(w_gate_up, expert_index, 0, keepdims=False)
        weights_gu = weights_gu.astype(jnp.float32).reshape(N_EXP, D // N_EXP, 2 * FF)
        split_rows = row_block.astype(jnp.float32).reshape(N_CTX * MOST, N_EXP, D // N_EXP)
        partial_sum = jnp.einsum('red,edf->ref', split_rows, weights_gu)
        summed = lax.optimization_barrier(jnp.sum(keep_round(partial_sum), axis=1))
        hidden_units = (jax.nn.silu(summed[:, :FF]) * summed[:, FF:]).astype(jnp.bfloat16)
        down_weight = lax.dynamic_index_in_dim(w_down, expert_index, 0, keepdims=False)
        result = jnp.dot(hidden_units, down_weight, preferred_element_type=jnp.float32).astype(jnp.bfloat16)
        moe_sum = moe_sum.at[tokens_for].add(weights_for[:, None] * result.astype(jnp.float32))
        return (moe_sum, active_for[0])
    moe_total = lax.scan(one_expert, jnp.zeros((SEQ, D), jnp.float32), jnp.arange(FLIGHT).astype(jnp.int32))[0]
    mixed = (hidden_state + moe_total).astype(jnp.bfloat16)
    return (context, mixed)
```

```python
import functools
import math

import jax
import jax.numpy as jnp
from jax import lax
from jax.experimental import pallas as pl
from jax.experimental.pallas import tpu as pltpu
from jax.sharding import Mesh, PartitionSpec as P

D = 4096
KVH = 2
TOPK = 8
MOST = 10
FLOOR = -1e20
EPSILON = 1e-06
CTX = ("y", "zl", "core")
EXP = ("zh", "x")
SIZES = {"y": 4, "zl": 8, "core": 2, "zh": 2, "x": 4}
F32 = jnp.float32
BF16 = jnp.bfloat16


def shift(value, axis, step):
    count = SIZES[axis]
    return lax.ppermute(value, axis, [(i, (i + step) % count) for i in range(count)])


def attend_kernel(place, q_ref, k_ref, v_ref, o_ref, *, heads, piece, tokens):
    rows = q_ref.shape[0]
    keys = k_ref.shape[0]
    half = keys // 2
    scores = lax.dot_general(
        k_ref[...], q_ref[...], (((1,), (1,)), ((), ())), preferred_element_type=F32
    )
    key = lax.broadcasted_iota(jnp.int32, (keys, rows), 0)
    row = lax.broadcasted_iota(jnp.int32, (keys, rows), 1) + pl.program_id(0) * rows
    core = jnp.where(key >= half, 1 - place[1], place[1])
    block = (key % half) // piece
    key_pos = (block * 2 + core) * tokens + place[2] * piece + key % piece
    row_pos = place[0] + row // heads
    factor = math.log2(math.e) / math.sqrt(q_ref.shape[1])
    masked = jnp.where(key_pos <= row_pos, scores * factor, -1e30)
    best = jnp.max(masked, axis=0, keepdims=True)
    best = jnp.maximum(best, FLOOR).astype(BF16)
    prob = jnp.exp2(masked - best.astype(F32))
    total = jnp.sum(prob, axis=0, keepdims=True)
    high = total.astype(BF16)
    low = (total - high.astype(F32)).astype(BF16)
    summed = lax.dot_general(
        v_ref[...], prob.astype(BF16), (((0,), (0,)), ((), ())), preferred_element_type=F32
    )
    size = v_ref.shape[1]
    o_ref[0:size, :] = summed.astype(BF16)
    line = lax.broadcasted_iota(jnp.int32, (16, rows), 0)
    extra = jnp.where(
        line == 0,
        best.astype(F32),
        jnp.where(line == 1, high.astype(F32), jnp.where(line == 2, low.astype(F32), 0.0)),
    )
    o_ref[size : size + 16, :] = extra.astype(BF16)


def attend(place, rows, keys, values, heads, piece, tokens):
    count, size = rows.shape
    step = 256
    return pl.pallas_call(
        functools.partial(attend_kernel, heads=heads, piece=piece, tokens=tokens),
        out_shape=jax.ShapeDtypeStruct((size + 16, count), BF16),
        grid=(count // step,),
        in_specs=[
            pl.BlockSpec(memory_space=pltpu.SMEM),
            pl.BlockSpec((step, size), lambda i: (i, 0)),
            pl.BlockSpec(keys.shape, lambda i: (0, 0)),
            pl.BlockSpec(values.shape, lambda i: (0, 0)),
        ],
        out_specs=pl.BlockSpec((size + 16, step), lambda i: (0, i)),
        compiler_params=pltpu.CompilerParams(vmem_limit_bytes=48 << 20),
        name="attend",
    )(place, rows, keys, values)


def body(queries, keys, values, resid, gain, expert_ids, gate_scores, w_gate_up, w_down, w_out):
    tokens, heads, size = queries.shape
    y, zl, core = lax.axis_index("y"), lax.axis_index("zl"), lax.axis_index("core")
    zh, x = lax.axis_index("zh"), lax.axis_index("x")
    ctx_place = (y * 8 + zl) * 2 + core
    ctx_count = 64
    width = resid.shape[1]

    whole_out = lax.all_gather(w_out, CTX, axis=1, tiled=True)

    piece = tokens // 4
    pair = jnp.stack([keys, values], axis=0)
    pair = lax.dynamic_index_in_dim(pair, zh, 2, keepdims=False)
    pair = lax.dynamic_slice_in_dim(pair, x * piece, piece, 1)
    pair = jnp.broadcast_to(pair[None], (8,) + pair.shape)
    pair = lax.all_to_all(pair, "zl", 0, 0, tiled=True)
    pair = jnp.broadcast_to(pair[None], (4,) + pair.shape)
    pair = lax.all_to_all(pair, "y", 0, 0, tiled=True)
    pair = jnp.stack([pair, shift(pair, "core", 1)], axis=0)
    all_keys = pair[:, :, :, 0].reshape(-1, size)
    all_values = pair[:, :, :, 1].reshape(-1, size)

    rows = queries.reshape(tokens * heads, size)
    place = jnp.stack([ctx_place * tokens, core, x]).astype(jnp.int32)
    asked = [shift(rows, "x", step) for step in (1, 2, 3)]
    parts = []
    for step in (2, 1, 3):
        found = attend(place, asked[step - 1], all_keys, all_values, heads, piece, tokens)
        parts.append(shift(found, "x", -step))
    parts.append(attend(place, rows, all_keys, all_values, heads, piece, tokens))

    bests = [part[size].astype(F32) for part in parts]
    best = functools.reduce(jnp.maximum, bests)
    above = jnp.zeros((size, tokens * heads), F32)
    below = jnp.zeros((tokens * heads,), F32)
    for part, top in zip(parts, bests):
        scale = jnp.exp2(top - best)
        above = above + part[:size].astype(F32) * scale[None, :]
        below = below + (part[size + 1].astype(F32) + part[size + 2].astype(F32)) * scale
    context = (above / below[None, :]).astype(BF16).T.reshape(tokens, heads, size)

    projected = jnp.dot(
        context.reshape(tokens, heads * size),
        whole_out.reshape(heads * size, D),
        preferred_element_type=F32,
    ).astype(BF16)
    projected = projected.reshape(tokens, 2, 4, width).transpose(2, 1, 0, 3)
    projected = lax.all_to_all(projected, "x", 0, 0, tiled=True)
    half = jnp.sum(projected.astype(F32), axis=0)
    theirs = lax.dynamic_index_in_dim(half, 1 - zh, 0, keepdims=False).astype(BF16)
    mine = lax.dynamic_index_in_dim(half, zh, 0, keepdims=False)
    attended = mine + shift(theirs, "zh", 1).astype(F32)
    state = resid.astype(F32) + attended
    scaled = (state * gain[None, :]).astype(BF16)

    slots = ctx_count * MOST
    ids = expert_ids.T
    expert = jnp.arange(ctx_count, dtype=jnp.int32)
    named = (ids[:, None, :] == expert[None, :, None]).astype(F32)
    weight = (gate_scores / jnp.sum(gate_scores, axis=1, keepdims=True)).T
    weight = jnp.sum(named * weight[:, None, :], axis=0)
    named = jnp.sum(named, axis=0).astype(BF16)
    token = jnp.arange(tokens, dtype=jnp.int32)
    before = (token[:, None] < token[None, :]).astype(BF16)
    rank = jnp.dot(named, before, preferred_element_type=F32)
    slot = jnp.arange(slots, dtype=jnp.int32)
    spread = (slot[:, None] // MOST == expert[None, :]).astype(BF16)
    weight_high = weight.astype(BF16)
    weight_low = (weight - weight_high.astype(F32)).astype(BF16)
    rank = jnp.where(named > 0, rank, -1.0).astype(BF16)
    tables = jnp.concatenate([rank, weight_high, weight_low], axis=1)
    tables = jnp.dot(spread, tables, preferred_element_type=F32)
    live = tables[:, :tokens] == (slot % MOST).astype(F32)[:, None]
    dispatch = live.astype(BF16)
    combine = jnp.concatenate(
        [
            jnp.where(live, tables[:, tokens : 2 * tokens], 0.0).astype(BF16),
            jnp.where(live, tables[:, 2 * tokens :], 0.0).astype(BF16),
        ],
        axis=1,
    )

    outgoing = jnp.dot(dispatch, scaled, preferred_element_type=F32).astype(BF16)
    outgoing = outgoing.reshape(ctx_count, MOST, width)
    arrived = lax.all_to_all(outgoing, CTX, 0, 0, tiled=True).reshape(slots, width)

    units = w_gate_up.shape[3]
    part = jnp.dot(
        arrived, w_gate_up.reshape(width, 2 * units), preferred_element_type=F32
    ).astype(BF16)
    plain = arrived.astype(F32) / gain[None, :]
    square = jnp.sum(plain * plain, axis=1, keepdims=True)
    high = square.astype(BF16)
    low = (square - high.astype(F32)).astype(BF16)
    lane = jnp.arange(128)[None, :]
    extra = jnp.where(lane == 0, high, jnp.where(lane == 1, low, jnp.zeros((), BF16)))
    part = jnp.concatenate([part, extra], axis=1)
    part = part.reshape(4, slots // 4, 2 * units + 128)
    part = lax.all_to_all(part, "x", 0, 0, tiled=True)
    part = jnp.sum(part.astype(F32), axis=0).reshape(2, slots // 8, 2 * units + 128)
    theirs = lax.dynamic_index_in_dim(part, 1 - zh, 0, keepdims=False).astype(BF16)
    mine = lax.dynamic_index_in_dim(part, zh, 0, keepdims=False)
    part = mine + shift(theirs, "zh", 1).astype(F32)
    square = part[:, 2 * units : 2 * units + 1] + part[:, 2 * units + 1 : 2 * units + 2]
    inverse = lax.rsqrt(square / D + EPSILON)
    hidden = (jax.nn.silu(part[:, :units] * inverse) * (part[:, units : 2 * units] * inverse)).astype(
        BF16
    )
    other = shift(hidden, "zh", 1)
    hidden = jnp.where(
        zh == 0, jnp.stack([hidden, other], axis=0), jnp.stack([other, hidden], axis=0)
    ).reshape(slots // 4, units)
    hidden = lax.all_gather(hidden, "x", axis=0, tiled=True)
    result = jnp.dot(hidden, w_down[0], preferred_element_type=F32).astype(BF16)
    result = result.reshape(ctx_count, MOST, width)
    returned = lax.all_to_all(result, CTX, 0, 0, tiled=True).reshape(slots, width)
    routed = lax.dot_general(
        combine, returned, (((0,), (0,)), ((), ())), preferred_element_type=F32
    )
    routed = routed[:tokens] + routed[tokens:]
    mixed = (state + routed).astype(BF16)
    return (context, mixed)


def solution(mesh):
    mesh = Mesh(mesh.devices.reshape(4, 8, 2, 2, 4), CTX + EXP)
    in_specs = (
        P(CTX, EXP, None),
        P(CTX, None, None),
        P(CTX, None, None),
        P(CTX, EXP),
        P(EXP),
        P(CTX, None),
        P(CTX, None),
        P(CTX, EXP, None, None),
        P(CTX, None, EXP),
        P(EXP, CTX, None),
    )
    out_specs = (P(CTX, EXP, None), P(CTX, EXP))
    return jax.shard_map(body, mesh=mesh, in_specs=in_specs, out_specs=out_specs, check_vma=False)
```

```python
import functools
import math

import jax
import jax.numpy as jnp
from jax import lax
from jax.experimental import pallas as pl
from jax.experimental.pallas import tpu as pltpu
from jax.sharding import Mesh, PartitionSpec as P

D = 4096
KVH = 2
TOPK = 8
MOST = 10
FLOOR = -1e20
EPSILON = 1e-06
CTX = ("y", "zl", "core")
EXP = ("zh", "x")
SIZES = {"y": 4, "zl": 8, "core": 2, "zh": 2, "x": 4}
F32 = jnp.float32
BF16 = jnp.bfloat16


def shift(value, axis, step):
    count = SIZES[axis]
    return lax.ppermute(value, axis, [(i, (i + step) % count) for i in range(count)])


def partner(value, axis, bit):
    return lax.ppermute(value, axis, [(i, i ^ bit) for i in range(SIZES[axis])])


def gather_out(w_out):
    rows = w_out.reshape(-1, D)
    for bit in (4, 2, 1):
        rows = jnp.concatenate([rows, partner(rows, "zl", bit)], axis=0)
    half = rows.shape[0] // 2
    below = shift(rows, "y", 1)
    above = shift(rows, "y", -1)
    across = [shift(below[:half], "y", 1), shift(above[half:], "y", -1)]
    near = jnp.concatenate([rows, below, above] + across, axis=0)
    return near, shift(near, "core", 1)


def feature_order(y, zl, core, heads, size):
    place = lax.broadcasted_iota(jnp.int32, (heads * size, heads * size), 1)
    source = lax.broadcasted_iota(jnp.int32, (heads * size, heads * size), 0)
    inner = place % (2 * heads)
    slot = place // (2 * heads)
    bits = slot % 8
    from_zl = zl ^ (bits // 4 + bits // 2 % 2 * 2 + bits % 2 * 4)
    turn = slot // 8 % 4
    from_y = (y + jnp.where(turn == 1, 3, jnp.where(turn == 2, 1, jnp.where(turn == 3, 2, 0)))) % 4
    from_core = jnp.where(slot >= 32, 1 - core, core)
    block = (from_y * 8 + from_zl) * 2 + from_core
    return (source == inner // 2 * size + block * 2 + inner % 2).astype(BF16)


def swap_order():
    count = 16 * MOST
    into = lax.broadcasted_iota(jnp.int32, (count, count), 0)
    source = lax.broadcasted_iota(jnp.int32, (count, count), 1)
    outer, inner, rank = into // (4 * MOST), into // MOST % 4, into % MOST
    return (source == (inner * 4 + outer) * MOST + rank).astype(BF16)


def gate_up_kernel(x_ref, order_ref, w_ref, gain_ref, o_ref, rows_ref):
    step = order_ref.shape[0]
    quarter = step // 4
    lanes = x_ref.shape[1]
    for b in range(x_ref.shape[0] // step):
        moved = jnp.dot(
            order_ref[...], x_ref[b * step : (b + 1) * step, :], preferred_element_type=F32
        ).astype(BF16)
        for c in range(4):
            rows_ref[b * quarter : (b + 1) * quarter, c * lanes : (c + 1) * lanes] = moved[
                c * quarter : (c + 1) * quarter
            ]
    wide = w_ref.shape[1]
    inverse = 1.0 / gain_ref[...]
    for b in range(rows_ref.shape[0] // step):
        rows = rows_ref[b * step : (b + 1) * step, :]
        part = jnp.dot(rows, w_ref[...], preferred_element_type=F32)
        o_ref[b * step : (b + 1) * step, 0:wide] = part.astype(BF16)
        plain = rows.astype(F32) * inverse
        square = jnp.sum(plain * plain, axis=1, keepdims=True)
        high = square.astype(BF16).astype(F32)
        lane = lax.broadcasted_iota(jnp.int32, (step, 128), 1)
        extra = jnp.where(lane == 0, high, jnp.where(lane == 1, square - high, 0.0))
        o_ref[b * step : (b + 1) * step, wide : wide + 128] = extra.astype(BF16)


def gate_up(arrived, weights, gain):
    slots = arrived.shape[0] // 4
    return pl.pallas_call(
        gate_up_kernel,
        out_shape=jax.ShapeDtypeStruct((slots, weights.shape[1] + 128), BF16),
        scratch_shapes=[pltpu.VMEM((slots, weights.shape[0]), BF16)],
        compiler_params=pltpu.CompilerParams(vmem_limit_bytes=48 << 20),
        name="gate_up",
    )(arrived, swap_order(), weights, gain[None, :])


def down_kernel(h_ref, order_ref, w_ref, o_ref):
    step = order_ref.shape[0]
    quarter = step // 4
    lanes = o_ref.shape[1]
    for a in range(h_ref.shape[0] // step):
        found = jnp.dot(
            h_ref[a * step : (a + 1) * step, :], w_ref[...], preferred_element_type=F32
        )
        for e in range(4):
            b = a * 4 + e
            piece = found[e * quarter : (e + 1) * quarter]
            piece = jnp.concatenate(
                [piece[:, c * lanes : (c + 1) * lanes] for c in range(4)], axis=0
            ).astype(BF16)
            o_ref[b * step : (b + 1) * step, :] = jnp.dot(
                order_ref[...], piece, preferred_element_type=F32
            ).astype(BF16)


def down(hidden, weights):
    lanes = weights.shape[1] // 4
    return pl.pallas_call(
        down_kernel,
        out_shape=jax.ShapeDtypeStruct((hidden.shape[0] * 4, lanes), BF16),
        compiler_params=pltpu.CompilerParams(vmem_limit_bytes=48 << 20),
        name="down",
    )(hidden, swap_order(), weights)


def attend_kernel(place, q_ref, k_ref, v_ref, o_ref, *, heads, piece, tokens):
    rows = q_ref.shape[0]
    keys = k_ref.shape[0]
    half = keys // 2
    scores = lax.dot_general(
        k_ref[...], q_ref[...], (((1,), (1,)), ((), ())), preferred_element_type=F32
    )
    key = lax.broadcasted_iota(jnp.int32, (keys, rows), 0)
    row = lax.broadcasted_iota(jnp.int32, (keys, rows), 1) + pl.program_id(0) * rows
    core = jnp.where(key >= half, 1 - place[1], place[1])
    block = (key % half) // piece
    key_pos = (block * 2 + core) * tokens + place[2] * piece + key % piece
    row_pos = place[0] + row // heads
    factor = math.log2(math.e) / math.sqrt(q_ref.shape[1])
    masked = jnp.where(key_pos <= row_pos, scores * factor, -1e30)
    best = jnp.max(masked, axis=0, keepdims=True)
    best = jnp.maximum(best, FLOOR).astype(BF16)
    prob = jnp.exp2(masked - best.astype(F32))
    total = jnp.sum(prob, axis=0, keepdims=True)
    high = total.astype(BF16)
    low = (total - high.astype(F32)).astype(BF16)
    summed = lax.dot_general(
        v_ref[...], prob.astype(BF16), (((0,), (0,)), ((), ())), preferred_element_type=F32
    )
    size = v_ref.shape[1]
    o_ref[0:size, :] = summed.astype(BF16)
    line = lax.broadcasted_iota(jnp.int32, (16, rows), 0)
    extra = jnp.where(
        line == 0,
        best.astype(F32),
        jnp.where(line == 1, high.astype(F32), jnp.where(line == 2, low.astype(F32), 0.0)),
    )
    o_ref[size : size + 16, :] = extra.astype(BF16)


def attend(place, rows, keys, values, heads, piece, tokens):
    count, size = rows.shape
    step = 256
    return pl.pallas_call(
        functools.partial(attend_kernel, heads=heads, piece=piece, tokens=tokens),
        out_shape=jax.ShapeDtypeStruct((size + 16, count), BF16),
        grid=(count // step,),
        in_specs=[
            pl.BlockSpec(memory_space=pltpu.SMEM),
            pl.BlockSpec((step, size), lambda i: (i, 0)),
            pl.BlockSpec(keys.shape, lambda i: (0, 0)),
            pl.BlockSpec(values.shape, lambda i: (0, 0)),
        ],
        out_specs=pl.BlockSpec((size + 16, step), lambda i: (0, i)),
        compiler_params=pltpu.CompilerParams(vmem_limit_bytes=48 << 20),
        name="attend",
    )(place, rows, keys, values)


def body(queries, keys, values, resid, gain, expert_ids, gate_scores, w_gate_up, w_down, w_out):
    tokens, heads, size = queries.shape
    y, zl, core = lax.axis_index("y"), lax.axis_index("zl"), lax.axis_index("core")
    zh, x = lax.axis_index("zh"), lax.axis_index("x")
    ctx_place = (y * 8 + zl) * 2 + core
    ctx_count = 64
    width = resid.shape[1]

    near, far = gather_out(w_out)

    piece = tokens // 4
    pair = jnp.stack([keys, values], axis=0)
    pair = lax.dynamic_index_in_dim(pair, zh, 2, keepdims=False)
    pair = lax.dynamic_slice_in_dim(pair, x * piece, piece, 1)
    pair = jnp.broadcast_to(pair[None], (8,) + pair.shape)
    pair = lax.all_to_all(pair, "zl", 0, 0, tiled=True)
    pair = jnp.broadcast_to(pair[None], (4,) + pair.shape)
    pair = lax.all_to_all(pair, "y", 0, 0, tiled=True)
    pair = jnp.stack([pair, shift(pair, "core", 1)], axis=0)
    all_keys = pair[:, :, :, 0].reshape(-1, size)
    all_values = pair[:, :, :, 1].reshape(-1, size)

    rows = queries.reshape(tokens * heads, size)
    place = jnp.stack([ctx_place * tokens, core, x]).astype(jnp.int32)
    asked = [shift(rows, "x", step) for step in (1, 2, 3)]
    parts = []
    for step in (2, 1, 3):
        found = attend(place, asked[step - 1], all_keys, all_values, heads, piece, tokens)
        parts.append(shift(found, "x", -step))
    parts.append(attend(place, rows, all_keys, all_values, heads, piece, tokens))

    bests = [part[size].astype(F32) for part in parts]
    best = functools.reduce(jnp.maximum, bests)
    above = jnp.zeros((size, tokens * heads), F32)
    below = jnp.zeros((tokens * heads,), F32)
    for part, top in zip(parts, bests):
        scale = jnp.exp2(top - best)
        above = above + part[:size].astype(F32) * scale[None, :]
        below = below + (part[size + 1].astype(F32) + part[size + 2].astype(F32)) * scale
    context = (above / below[None, :]).astype(BF16).T.reshape(tokens, heads, size)

    order = feature_order(y, zl, core, heads, size)
    ordered = jnp.dot(
        context.reshape(tokens, heads * size), order, preferred_element_type=F32
    ).astype(BF16)
    split = heads * size // 2
    projected = jnp.dot(ordered[:, :split], near, preferred_element_type=F32)
    projected = projected + jnp.dot(ordered[:, split:], far, preferred_element_type=F32)
    projected = projected.astype(BF16)
    projected = projected.reshape(tokens, 2, 4, width).transpose(2, 1, 0, 3)
    projected = lax.all_to_all(projected, "x", 0, 0, tiled=True)
    half = jnp.sum(projected.astype(F32), axis=0)
    theirs = lax.dynamic_index_in_dim(half, 1 - zh, 0, keepdims=False).astype(BF16)
    mine = lax.dynamic_index_in_dim(half, zh, 0, keepdims=False)
    attended = mine + shift(theirs, "zh", 1).astype(F32)
    state = resid.astype(F32) + attended
    scaled = (state * gain[None, :]).astype(BF16)

    slots = ctx_count * MOST
    ids = expert_ids.T
    expert = jnp.arange(ctx_count, dtype=jnp.int32)
    named = (ids[:, None, :] == expert[None, :, None]).astype(F32)
    weight = (gate_scores / jnp.sum(gate_scores, axis=1, keepdims=True)).T
    weight = jnp.sum(named * weight[:, None, :], axis=0)
    named = jnp.sum(named, axis=0).astype(BF16)
    token = jnp.arange(tokens, dtype=jnp.int32)
    before = (token[:, None] < token[None, :]).astype(BF16)
    rank = jnp.dot(named, before, preferred_element_type=F32)
    line = jnp.arange(4 * slots, dtype=jnp.int32)
    spread = (line[:, None] // (4 * MOST) == expert[None, :]).astype(BF16)
    weight_high = weight.astype(BF16)
    weight_low = (weight - weight_high.astype(F32)).astype(BF16)
    rank = jnp.where(named > 0, rank, -1.0).astype(BF16)
    tables = jnp.concatenate([rank, weight_high, weight_low], axis=1)
    tables = jnp.dot(spread, tables, preferred_element_type=F32)
    live = tables[:, :tokens] == (line % MOST).astype(F32)[:, None]
    chunk = line // MOST % 4

    def by_chunk(table):
        table = table.astype(BF16)
        zero = jnp.zeros((), BF16)
        return [jnp.where((chunk == c)[:, None], table, zero) for c in range(4)]

    dispatch = jnp.concatenate(by_chunk(live), axis=1)
    combine = jnp.concatenate(
        by_chunk(jnp.where(live, tables[:, tokens : 2 * tokens], 0.0))
        + by_chunk(jnp.where(live, tables[:, 2 * tokens :], 0.0)),
        axis=1,
    )

    lanes = width // 4
    stacked = jnp.concatenate([scaled[:, c * lanes : (c + 1) * lanes] for c in range(4)], axis=0)
    outgoing = jnp.dot(dispatch, stacked, preferred_element_type=F32).astype(BF16)
    outgoing = outgoing.reshape(ctx_count, 4 * MOST, lanes)
    arrived = lax.all_to_all(outgoing, CTX, 0, 0, tiled=True).reshape(4 * slots, lanes)

    units = w_gate_up.shape[3]
    part = gate_up(arrived, w_gate_up.reshape(width, 2 * units), gain)
    part = part.reshape(4, slots // 4, 2 * units + 128)
    part = lax.all_to_all(part, "x", 0, 0, tiled=True)
    part = jnp.sum(part.astype(F32), axis=0).reshape(2, slots // 8, 2 * units + 128)
    theirs = lax.dynamic_index_in_dim(part, 1 - zh, 0, keepdims=False).astype(BF16)
    mine = lax.dynamic_index_in_dim(part, zh, 0, keepdims=False)
    part = mine + shift(theirs, "zh", 1).astype(F32)
    square = part[:, 2 * units : 2 * units + 1] + part[:, 2 * units + 1 : 2 * units + 2]
    inverse = lax.rsqrt(square / D + EPSILON)
    hidden = (jax.nn.silu(part[:, :units] * inverse) * (part[:, units : 2 * units] * inverse)).astype(
        BF16
    )
    other = shift(hidden, "zh", 1)
    hidden = jnp.where(
        zh == 0, jnp.stack([hidden, other], axis=0), jnp.stack([other, hidden], axis=0)
    ).reshape(slots // 4, units)
    hidden = lax.all_gather(hidden, "x", axis=0, tiled=True)
    result = down(hidden, w_down[0]).reshape(ctx_count, 4 * MOST, lanes)
    returned = lax.all_to_all(result, CTX, 0, 0, tiled=True).reshape(4 * slots, lanes)
    routed = lax.dot_general(
        combine, returned, (((0,), (0,)), ((), ())), preferred_element_type=F32
    )
    routed = routed[: 4 * tokens] + routed[4 * tokens :]
    routed = jnp.concatenate([routed[c * tokens : (c + 1) * tokens] for c in range(4)], axis=1)
    mixed = (state + routed).astype(BF16)
    return (context, mixed)


def solution(mesh):
    mesh = Mesh(mesh.devices.reshape(4, 8, 2, 2, 4), CTX + EXP)
    in_specs = (
        P(CTX, EXP, None),
        P(CTX, None, None),
        P(CTX, None, None),
        P(CTX, EXP),
        P(EXP),
        P(CTX, None),
        P(CTX, None),
        P(CTX, EXP, None, None),
        P(CTX, None, EXP),
        P(EXP, CTX, None),
    )
    out_specs = (P(CTX, EXP, None), P(CTX, EXP))
    return jax.shard_map(body, mesh=mesh, in_specs=in_specs, out_specs=out_specs, check_vma=False)
```

```python
import functools
import math

import jax
import jax.numpy as jnp
from jax import lax
from jax.experimental import pallas as pl
from jax.experimental.pallas import tpu as pltpu
from jax.sharding import Mesh, PartitionSpec as P

D = 4096
KVH = 2
TOPK = 8
MOST = 10
FLOOR = -1e20
EPSILON = 1e-06
CTX = ("y", "zl", "core")
EXP = ("zh", "x")
SIZES = {"y": 4, "zl": 8, "core": 2, "zh": 2, "x": 4}
F32 = jnp.float32
BF16 = jnp.bfloat16


def shift(value, axis, step):
    count = SIZES[axis]
    return lax.ppermute(value, axis, [(i, (i + step) % count) for i in range(count)])


def partner(value, axis, bit):
    return lax.ppermute(value, axis, [(i, i ^ bit) for i in range(SIZES[axis])])


def after(value, earlier):
    return lax.optimization_barrier((value, earlier))[0]


def gather_line(w_out):
    rows = w_out.reshape(-1, D)
    rows = jnp.concatenate([rows, partner(rows, "zl", 4)], axis=0)
    return jnp.concatenate([rows, partner(rows, "zl", 2)], axis=0)


def gather_rest(rows, first, second):
    rows = after(rows, first)
    rows = jnp.concatenate([rows, partner(rows, "zl", 1)], axis=0)
    rows = after(rows, second)
    rows = jnp.broadcast_to(rows[None], (4,) + rows.shape)
    return lax.all_to_all(rows, "y", 0, 0, tiled=True).reshape(-1, D)


def feature_order(zl, core, heads, size):
    place = lax.broadcasted_iota(jnp.int32, (heads * size, heads * size), 1)
    source = lax.broadcasted_iota(jnp.int32, (heads * size, heads * size), 0)
    inner = place % (2 * heads)
    slot = place // (2 * heads)
    bits = slot % 8
    from_zl = zl ^ (bits // 4 + bits // 2 % 2 * 2 + bits % 2 * 4)
    from_core = jnp.where(slot >= 32, 1 - core, core)
    block = (slot // 8 % 4 * 8 + from_zl) * 2 + from_core
    return (source == inner // 2 * size + block * 2 + inner % 2).astype(BF16)


def project_kernel(c_ref, near_ref, far_ref, o_ref):
    half = near_ref.shape[0]
    part = jnp.dot(c_ref[:, :half], near_ref[...], preferred_element_type=F32)
    part = part + jnp.dot(c_ref[:, half:], far_ref[...], preferred_element_type=F32)
    o_ref[0, 0] = part.astype(BF16)


def project(ordered, near, far):
    tokens = ordered.shape[0]
    width = D // 8
    return pl.pallas_call(
        project_kernel,
        out_shape=jax.ShapeDtypeStruct((4, 2, tokens, width), BF16),
        grid=(4, 2),
        in_specs=[
            pl.BlockSpec(ordered.shape, lambda i, j: (0, 0)),
            pl.BlockSpec((near.shape[0], width), lambda i, j: (0, j * 4 + i)),
            pl.BlockSpec((near.shape[0], width), lambda i, j: (0, j * 4 + i)),
        ],
        out_specs=pl.BlockSpec((1, 1, tokens, width), lambda i, j: (i, j, 0, 0)),
        compiler_params=pltpu.CompilerParams(vmem_limit_bytes=32 << 20),
        name="project",
    )(ordered, near, far)


def swap_order():
    count = 16 * MOST
    into = lax.broadcasted_iota(jnp.int32, (count, count), 0)
    source = lax.broadcasted_iota(jnp.int32, (count, count), 1)
    outer, inner, rank = into // (4 * MOST), into // MOST % 4, into % MOST
    return (source == (inner * 4 + outer) * MOST + rank).astype(BF16)


def gate_up_kernel(x_ref, order_ref, w_ref, gain_ref, o_ref, rows_ref):
    step = order_ref.shape[0]
    quarter = step // 4
    lanes = x_ref.shape[1]
    for b in range(x_ref.shape[0] // step):
        moved = jnp.dot(
            order_ref[...], x_ref[b * step : (b + 1) * step, :], preferred_element_type=F32
        ).astype(BF16)
        for c in range(4):
            rows_ref[b * quarter : (b + 1) * quarter, c * lanes : (c + 1) * lanes] = moved[
                c * quarter : (c + 1) * quarter
            ]
    wide = w_ref.shape[1]
    inverse = 1.0 / gain_ref[...]
    for b in range(rows_ref.shape[0] // step):
        rows = rows_ref[b * step : (b + 1) * step, :]
        part = jnp.dot(rows, w_ref[...], preferred_element_type=F32)
        o_ref[b * step : (b + 1) * step, 0:wide] = part.astype(BF16)
        plain = rows.astype(F32) * inverse
        square = jnp.sum(plain * plain, axis=1, keepdims=True)
        high = square.astype(BF16).astype(F32)
        lane = lax.broadcasted_iota(jnp.int32, (step, 128), 1)
        extra = jnp.where(lane == 0, high, jnp.where(lane == 1, square - high, 0.0))
        o_ref[b * step : (b + 1) * step, wide : wide + 128] = extra.astype(BF16)


def gate_up(arrived, weights, gain):
    slots = arrived.shape[0] // 4
    return pl.pallas_call(
        gate_up_kernel,
        out_shape=jax.ShapeDtypeStruct((slots, weights.shape[1] + 128), BF16),
        scratch_shapes=[pltpu.VMEM((slots, weights.shape[0]), BF16)],
        compiler_params=pltpu.CompilerParams(vmem_limit_bytes=48 << 20),
        name="gate_up",
    )(arrived, swap_order(), weights, gain[None, :])


def down_kernel(h_ref, order_ref, w_ref, o_ref):
    step = order_ref.shape[0]
    quarter = step // 4
    lanes = o_ref.shape[1]
    for a in range(h_ref.shape[0] // step):
        found = jnp.dot(
            h_ref[a * step : (a + 1) * step, :], w_ref[...], preferred_element_type=F32
        )
        for e in range(4):
            b = a * 4 + e
            piece = found[e * quarter : (e + 1) * quarter]
            piece = jnp.concatenate(
                [piece[:, c * lanes : (c + 1) * lanes] for c in range(4)], axis=0
            ).astype(BF16)
            o_ref[b * step : (b + 1) * step, :] = jnp.dot(
                order_ref[...], piece, preferred_element_type=F32
            ).astype(BF16)


def down(hidden, weights):
    lanes = weights.shape[1] // 4
    return pl.pallas_call(
        down_kernel,
        out_shape=jax.ShapeDtypeStruct((hidden.shape[0] * 4, lanes), BF16),
        compiler_params=pltpu.CompilerParams(vmem_limit_bytes=48 << 20),
        name="down",
    )(hidden, swap_order(), weights)


def attend_kernel(place, q_ref, k_ref, v_ref, o_ref, *, heads, piece, tokens):
    rows = q_ref.shape[0]
    keys = k_ref.shape[0]
    half = keys // 2
    scores = lax.dot_general(
        k_ref[...], q_ref[...], (((1,), (1,)), ((), ())), preferred_element_type=F32
    )
    key = lax.broadcasted_iota(jnp.int32, (keys, rows), 0)
    row = lax.broadcasted_iota(jnp.int32, (keys, rows), 1) + pl.program_id(0) * rows
    core = jnp.where(key >= half, 1 - place[1], place[1])
    block = (key % half) // piece
    key_pos = (block * 2 + core) * tokens + place[2] * piece + key % piece
    row_pos = place[0] + row // heads
    factor = math.log2(math.e) / math.sqrt(q_ref.shape[1])
    masked = jnp.where(key_pos <= row_pos, scores * factor, -1e30)
    best = jnp.max(masked, axis=0, keepdims=True)
    best = jnp.maximum(best, FLOOR).astype(BF16)
    prob = jnp.exp2(masked - best.astype(F32))
    total = jnp.sum(prob, axis=0, keepdims=True)
    high = total.astype(BF16)
    low = (total - high.astype(F32)).astype(BF16)
    summed = lax.dot_general(
        v_ref[...], prob.astype(BF16), (((0,), (0,)), ((), ())), preferred_element_type=F32
    )
    size = v_ref.shape[1]
    o_ref[0:size, :] = summed.astype(BF16)
    line = lax.broadcasted_iota(jnp.int32, (16, rows), 0)
    extra = jnp.where(
        line == 0,
        best.astype(F32),
        jnp.where(line == 1, high.astype(F32), jnp.where(line == 2, low.astype(F32), 0.0)),
    )
    o_ref[size : size + 16, :] = extra.astype(BF16)


def attend(place, rows, keys, values, heads, piece, tokens):
    count, size = rows.shape
    step = 256
    return pl.pallas_call(
        functools.partial(attend_kernel, heads=heads, piece=piece, tokens=tokens),
        out_shape=jax.ShapeDtypeStruct((size + 16, count), BF16),
        grid=(count // step,),
        in_specs=[
            pl.BlockSpec(memory_space=pltpu.SMEM),
            pl.BlockSpec((step, size), lambda i: (i, 0)),
            pl.BlockSpec(keys.shape, lambda i: (0, 0)),
            pl.BlockSpec(values.shape, lambda i: (0, 0)),
        ],
        out_specs=pl.BlockSpec((size + 16, step), lambda i: (0, i)),
        compiler_params=pltpu.CompilerParams(vmem_limit_bytes=48 << 20),
        name="attend",
    )(place, rows, keys, values)


def body(queries, keys, values, resid, gain, expert_ids, gate_scores, w_gate_up, w_down, w_out):
    tokens, heads, size = queries.shape
    y, zl, core = lax.axis_index("y"), lax.axis_index("zl"), lax.axis_index("core")
    zh, x = lax.axis_index("zh"), lax.axis_index("x")
    ctx_place = (y * 8 + zl) * 2 + core
    ctx_count = 64
    width = resid.shape[1]

    piece = tokens // 4
    pair = jnp.stack([keys, values], axis=0)
    pair = lax.dynamic_index_in_dim(pair, zh, 2, keepdims=False)
    pair = lax.dynamic_slice_in_dim(pair, x * piece, piece, 1)
    pair = jnp.broadcast_to(pair[None], (8,) + pair.shape)
    line = gather_line(w_out)
    pair = first = lax.all_to_all(pair, "zl", 0, 0, tiled=True)
    rows = queries.reshape(tokens * heads, size)
    asked = [shift(rows, "x", step) for step in (1, 2, 3)]
    pair = after(pair, asked)
    pair = jnp.broadcast_to(pair[None], (4,) + pair.shape)
    pair = second = lax.all_to_all(pair, "y", 0, 0, tiled=True)
    near = gather_rest(line, first, second)
    pair = jnp.stack([pair, shift(pair, "core", 1)], axis=0)
    all_keys = pair[:, :, :, 0].reshape(-1, size)
    all_values = pair[:, :, :, 1].reshape(-1, size)

    place = jnp.stack([ctx_place * tokens, core, x]).astype(jnp.int32)
    parts, found = [], place
    for step in (2, 1, 3):
        theirs = after(asked[step - 1], found)
        found = attend(place, theirs, all_keys, all_values, heads, piece, tokens)
        parts.append(shift(found, "x", -step))
    rows = after(rows, found)
    parts.append(attend(place, rows, all_keys, all_values, heads, piece, tokens))
    near = after(near, parts)
    far = shift(near, "core", 1)

    bests = [part[size].astype(F32) for part in parts]
    best = functools.reduce(jnp.maximum, bests)
    above = jnp.zeros((size, tokens * heads), F32)
    below = jnp.zeros((tokens * heads,), F32)
    for part, top in zip(parts, bests):
        scale = jnp.exp2(top - best)
        above = above + part[:size].astype(F32) * scale[None, :]
        below = below + (part[size + 1].astype(F32) + part[size + 2].astype(F32)) * scale
    context = (above / below[None, :]).astype(BF16).T.reshape(tokens, heads, size)

    order = feature_order(zl, core, heads, size)
    ordered = jnp.dot(
        context.reshape(tokens, heads * size), order, preferred_element_type=F32
    ).astype(BF16)
    projected = project(ordered, near, far)
    projected = lax.all_to_all(projected, "x", 0, 0, tiled=True)
    half = jnp.sum(projected.astype(F32), axis=0)
    theirs = lax.dynamic_index_in_dim(half, 1 - zh, 0, keepdims=False).astype(BF16)
    mine = lax.dynamic_index_in_dim(half, zh, 0, keepdims=False)
    attended = mine + shift(theirs, "zh", 1).astype(F32)
    state = resid.astype(F32) + attended
    scaled = (state * gain[None, :]).astype(BF16)

    slots = ctx_count * MOST
    ids = expert_ids.T
    expert = jnp.arange(ctx_count, dtype=jnp.int32)
    named = (ids[:, None, :] == expert[None, :, None]).astype(F32)
    weight = (gate_scores / jnp.sum(gate_scores, axis=1, keepdims=True)).T
    weight = jnp.sum(named * weight[:, None, :], axis=0)
    named = jnp.sum(named, axis=0).astype(BF16)
    token = jnp.arange(tokens, dtype=jnp.int32)
    before = (token[:, None] < token[None, :]).astype(BF16)
    rank = jnp.dot(named, before, preferred_element_type=F32)
    line = jnp.arange(4 * slots, dtype=jnp.int32)
    spread = (line[:, None] // (4 * MOST) == expert[None, :]).astype(BF16)
    weight_high = weight.astype(BF16)
    weight_low = (weight - weight_high.astype(F32)).astype(BF16)
    rank = jnp.where(named > 0, rank, -1.0).astype(BF16)
    tables = jnp.concatenate([rank, weight_high, weight_low], axis=1)
    tables = jnp.dot(spread, tables, preferred_element_type=F32)
    live = tables[:, :tokens] == (line % MOST).astype(F32)[:, None]
    chunk = line // MOST % 4

    def by_chunk(table):
        table = table.astype(BF16)
        zero = jnp.zeros((), BF16)
        return [jnp.where((chunk == c)[:, None], table, zero) for c in range(4)]

    dispatch = jnp.concatenate(by_chunk(live), axis=1)
    combine = jnp.concatenate(
        by_chunk(jnp.where(live, tables[:, tokens : 2 * tokens], 0.0))
        + by_chunk(jnp.where(live, tables[:, 2 * tokens :], 0.0)),
        axis=1,
    )

    lanes = width // 4
    stacked = jnp.concatenate([scaled[:, c * lanes : (c + 1) * lanes] for c in range(4)], axis=0)
    outgoing = jnp.dot(dispatch, stacked, preferred_element_type=F32).astype(BF16)
    outgoing = outgoing.reshape(ctx_count, 4 * MOST, lanes)
    arrived = lax.all_to_all(outgoing, CTX, 0, 0, tiled=True).reshape(4 * slots, lanes)

    units = w_gate_up.shape[3]
    part = gate_up(arrived, w_gate_up.reshape(width, 2 * units), gain)
    part = part.reshape(4, slots // 4, 2 * units + 128)
    part = lax.all_to_all(part, "x", 0, 0, tiled=True)
    part = jnp.sum(part.astype(F32), axis=0).reshape(2, slots // 8, 2 * units + 128)
    theirs = lax.dynamic_index_in_dim(part, 1 - zh, 0, keepdims=False).astype(BF16)
    mine = lax.dynamic_index_in_dim(part, zh, 0, keepdims=False)
    part = mine + shift(theirs, "zh", 1).astype(F32)
    square = part[:, 2 * units : 2 * units + 1] + part[:, 2 * units + 1 : 2 * units + 2]
    inverse = lax.rsqrt(square / D + EPSILON)
    hidden = (jax.nn.silu(part[:, :units] * inverse) * (part[:, units : 2 * units] * inverse)).astype(
        BF16
    )
    other = shift(hidden, "zh", 1)
    hidden = jnp.where(
        zh == 0, jnp.stack([hidden, other], axis=0), jnp.stack([other, hidden], axis=0)
    ).reshape(slots // 4, units)
    hidden = lax.all_gather(hidden, "x", axis=0, tiled=True)
    result = down(hidden, w_down[0]).reshape(ctx_count, 4 * MOST, lanes)
    returned = lax.all_to_all(result, CTX, 0, 0, tiled=True).reshape(4 * slots, lanes)
    routed = lax.dot_general(
        combine, returned, (((0,), (0,)), ((), ())), preferred_element_type=F32
    )
    routed = routed[: 4 * tokens] + routed[4 * tokens :]
    routed = jnp.concatenate([routed[c * tokens : (c + 1) * tokens] for c in range(4)], axis=1)
    mixed = (state + routed).astype(BF16)
    return (context, mixed)


def solution(mesh):
    mesh = Mesh(mesh.devices.reshape(4, 8, 2, 2, 4), CTX + EXP)
    in_specs = (
        P(CTX, EXP, None),
        P(CTX, None, None),
        P(CTX, None, None),
        P(CTX, EXP),
        P(EXP),
        P(CTX, None),
        P(CTX, None),
        P(CTX, EXP, None, None),
        P(CTX, None, EXP),
        P(EXP, CTX, None),
    )
    out_specs = (P(CTX, EXP, None), P(CTX, EXP))
    return jax.shard_map(body, mesh=mesh, in_specs=in_specs, out_specs=out_specs, check_vma=False)
```

```python
import functools
import math

import jax
import jax.numpy as jnp
from jax import lax
from jax.experimental import pallas as pl
from jax.experimental.pallas import tpu as pltpu
from jax.sharding import Mesh, PartitionSpec as P

D = 4096
KVH = 2
TOPK = 8
MOST = 10
FLOOR = -1e20
EPSILON = 1e-06
CTX = ("y", "zl", "core")
EXP = ("zh", "x")
SIZES = {"y": 4, "zl": 8, "core": 2, "zh": 2, "x": 4}
F32 = jnp.float32
BF16 = jnp.bfloat16


def shift(value, axis, step):
    count = SIZES[axis]
    return lax.ppermute(value, axis, [(i, (i + step) % count) for i in range(count)])


def partner(value, axis, bit):
    return lax.ppermute(value, axis, [(i, i ^ bit) for i in range(SIZES[axis])])


def after(value, earlier):
    return lax.optimization_barrier((value, earlier))[0]


def double(rows, bit, earlier):
    rows = after(rows, earlier)
    return jnp.concatenate([rows, partner(rows, "zl", bit)], axis=0)


def feature_order(zl, core, heads, size):
    place = lax.broadcasted_iota(jnp.int32, (heads * size, heads * size), 1)
    source = lax.broadcasted_iota(jnp.int32, (heads * size, heads * size), 0)
    inner = place % (2 * heads)
    slot = place // (2 * heads)
    bits = slot % 8
    from_zl = zl ^ (bits // 4 + bits // 2 % 2 * 2 + bits % 2 * 4)
    from_core = jnp.where(slot >= 32, 1 - core, core)
    block = (slot // 8 % 4 * 8 + from_zl) * 2 + from_core
    return (source == inner // 2 * size + block * 2 + inner % 2).astype(BF16)


def project_kernel(side, c_ref, near_ref, far_ref, o_ref):
    half = near_ref.shape[0]
    part = jnp.dot(c_ref[:, :half], near_ref[...], preferred_element_type=F32)
    part = part + jnp.dot(c_ref[:, half:], far_ref[...], preferred_element_type=F32)
    o_ref[0] = part.astype(BF16)


def project(side, ordered, near, far):
    tokens = ordered.shape[0]
    width = D // 8
    return pl.pallas_call(
        project_kernel,
        out_shape=jax.ShapeDtypeStruct((4, tokens, width), BF16),
        grid_spec=pltpu.PrefetchScalarGridSpec(
            num_scalar_prefetch=1,
            grid=(4,),
            in_specs=[
                pl.BlockSpec(ordered.shape, lambda i, side: (0, 0)),
                pl.BlockSpec((near.shape[0], width), lambda i, side: (0, side[0] * 4 + i)),
                pl.BlockSpec((near.shape[0], width), lambda i, side: (0, side[0] * 4 + i)),
            ],
            out_specs=pl.BlockSpec((1, tokens, width), lambda i, side: (i, 0, 0)),
        ),
        compiler_params=pltpu.CompilerParams(vmem_limit_bytes=32 << 20),
        name="project",
    )(side, ordered, near, far)


def sum_along_x(parts):
    return jnp.sum(lax.all_to_all(parts, "x", 0, 0, tiled=True).astype(F32), axis=0)


def swap_order():
    count = 16 * MOST
    into = lax.broadcasted_iota(jnp.int32, (count, count), 0)
    source = lax.broadcasted_iota(jnp.int32, (count, count), 1)
    outer, inner, rank = into // (4 * MOST), into // MOST % 4, into % MOST
    return (source == (inner * 4 + outer) * MOST + rank).astype(BF16)


def gate_up_kernel(side, x_ref, order_ref, w_ref, gain_ref, o_ref, rows_ref):
    step = order_ref.shape[0]
    begin = pl.multiple_of(side[0] * (x_ref.shape[0] // 2), 16)
    quarter = step // 4
    lanes = x_ref.shape[1]
    for b in range(x_ref.shape[0] // step // 2):
        moved = jnp.dot(
            order_ref[...], x_ref[pl.ds(begin + b * step, step), :], preferred_element_type=F32
        ).astype(BF16)
        for c in range(4):
            rows_ref[b * quarter : (b + 1) * quarter, c * lanes : (c + 1) * lanes] = moved[
                c * quarter : (c + 1) * quarter
            ]
    wide = w_ref.shape[1]
    inverse = 1.0 / gain_ref[...]
    step = step // 2
    for b in range(rows_ref.shape[0] // step):
        rows = rows_ref[b * step : (b + 1) * step, :]
        part = jnp.dot(rows, w_ref[...], preferred_element_type=F32)
        o_ref[b * step : (b + 1) * step, 0:wide] = part.astype(BF16)
        plain = rows.astype(F32) * inverse
        square = jnp.sum(plain * plain, axis=1, keepdims=True)
        high = square.astype(BF16).astype(F32)
        lane = lax.broadcasted_iota(jnp.int32, (step, 128), 1)
        extra = jnp.where(lane == 0, high, jnp.where(lane == 1, square - high, 0.0))
        o_ref[b * step : (b + 1) * step, wide : wide + 128] = extra.astype(BF16)


def gate_up(side, arrived, order, weights, gain):
    slots = arrived.shape[0] // 8
    return pl.pallas_call(
        gate_up_kernel,
        out_shape=jax.ShapeDtypeStruct((slots, weights.shape[1] + 128), BF16),
        in_specs=[pl.BlockSpec(memory_space=pltpu.SMEM)] + [pl.BlockSpec(memory_space=pltpu.VMEM)] * 4,
        scratch_shapes=[pltpu.VMEM((slots, weights.shape[0]), BF16)],
        compiler_params=pltpu.CompilerParams(vmem_limit_bytes=48 << 20),
        name="gate_up",
    )(side, arrived, order, weights, gain[None, :])


def down_kernel(h_ref, order_ref, w_ref, o_ref):
    step = order_ref.shape[0]
    quarter = step // 4
    lanes = o_ref.shape[1]
    for a in range(h_ref.shape[0] // step):
        found = jnp.dot(
            h_ref[a * step : (a + 1) * step, :], w_ref[...], preferred_element_type=F32
        )
        for e in range(4):
            b = e // 2 * 8 + a * 2 + e % 2
            piece = found[e * quarter : (e + 1) * quarter]
            piece = jnp.concatenate(
                [piece[:, c * lanes : (c + 1) * lanes] for c in range(4)], axis=0
            ).astype(BF16)
            o_ref[b * step : (b + 1) * step, :] = jnp.dot(
                order_ref[...], piece, preferred_element_type=F32
            ).astype(BF16)


def down(hidden, order, weights):
    lanes = weights.shape[1] // 4
    return pl.pallas_call(
        down_kernel,
        out_shape=jax.ShapeDtypeStruct((hidden.shape[0] * 4, lanes), BF16),
        compiler_params=pltpu.CompilerParams(vmem_limit_bytes=48 << 20),
        name="down",
    )(hidden, order, weights)


def attend_kernel(place, q_ref, k_ref, v_ref, o_ref, *, heads, piece, tokens):
    rows = q_ref.shape[0]
    keys = k_ref.shape[0]
    half = keys // 2
    scores = lax.dot_general(
        k_ref[...], q_ref[...], (((1,), (1,)), ((), ())), preferred_element_type=F32
    )
    key = lax.broadcasted_iota(jnp.int32, (keys, rows), 0)
    row = lax.broadcasted_iota(jnp.int32, (keys, rows), 1) + pl.program_id(0) * rows
    core = jnp.where(key >= half, 1 - place[1], place[1])
    block = (key % half) // piece
    key_pos = (block * 2 + core) * tokens + place[2] * piece + key % piece
    row_pos = place[0] + row // heads
    factor = math.log2(math.e) / math.sqrt(q_ref.shape[1])
    masked = jnp.where(key_pos <= row_pos, scores * factor, -1e30)
    best = jnp.max(masked, axis=0, keepdims=True)
    best = jnp.maximum(best, FLOOR).astype(BF16)
    prob = jnp.exp2(masked - best.astype(F32))
    total = jnp.sum(prob, axis=0, keepdims=True)
    high = total.astype(BF16)
    low = (total - high.astype(F32)).astype(BF16)
    summed = lax.dot_general(
        v_ref[...], prob.astype(BF16), (((0,), (0,)), ((), ())), preferred_element_type=F32
    )
    size = v_ref.shape[1]
    o_ref[0:size, :] = summed.astype(BF16)
    line = lax.broadcasted_iota(jnp.int32, (16, rows), 0)
    extra = jnp.where(
        line == 0,
        best.astype(F32),
        jnp.where(line == 1, high.astype(F32), jnp.where(line == 2, low.astype(F32), 0.0)),
    )
    o_ref[size : size + 16, :] = extra.astype(BF16)


def attend(place, rows, keys, values, heads, piece, tokens):
    count, size = rows.shape
    step = 256
    return pl.pallas_call(
        functools.partial(attend_kernel, heads=heads, piece=piece, tokens=tokens),
        out_shape=jax.ShapeDtypeStruct((size + 16, count), BF16),
        grid=(count // step,),
        in_specs=[
            pl.BlockSpec(memory_space=pltpu.SMEM),
            pl.BlockSpec((step, size), lambda i: (i, 0)),
            pl.BlockSpec(keys.shape, lambda i: (0, 0)),
            pl.BlockSpec(values.shape, lambda i: (0, 0)),
        ],
        out_specs=pl.BlockSpec((size + 16, step), lambda i: (0, i)),
        compiler_params=pltpu.CompilerParams(vmem_limit_bytes=48 << 20),
        name="attend",
    )(place, rows, keys, values)


def body(queries, keys, values, resid, gain, expert_ids, gate_scores, w_gate_up, w_down, w_out):
    tokens, heads, size = queries.shape
    y, zl, core = lax.axis_index("y"), lax.axis_index("zl"), lax.axis_index("core")
    zh, x = lax.axis_index("zh"), lax.axis_index("x")
    ctx_place = (y * 8 + zl) * 2 + core
    ctx_count = 64
    width = resid.shape[1]

    piece = tokens // 4
    pair = jnp.stack([keys, values], axis=0)
    pair = lax.dynamic_index_in_dim(pair, zh, 2, keepdims=False)
    pair = lax.dynamic_slice_in_dim(pair, x * piece, piece, 1)
    pair = jnp.broadcast_to(pair[None], (8,) + pair.shape)
    line = w_out.reshape(-1, D)
    line = jnp.concatenate([line, partner(line, "zl", 4)], axis=0)
    pair = first = lax.all_to_all(pair, "zl", 0, 0, tiled=True)
    rows = queries.reshape(tokens * heads, size)
    asked = [shift(rows, "x", step) for step in (1, 2, 3)]
    pair = after(pair, asked)
    pair = jnp.broadcast_to(pair[None], (4,) + pair.shape)
    pair = second = lax.all_to_all(pair, "y", 0, 0, tiled=True)
    line = double(line, 2, first)
    line = double(line, 1, second)
    pair = jnp.stack([pair, shift(pair, "core", 1)], axis=0)
    all_keys = pair[:, :, :, 0].reshape(-1, size)
    all_values = pair[:, :, :, 1].reshape(-1, size)

    place = jnp.stack([ctx_place * tokens, core, x]).astype(jnp.int32)
    parts, found = [], place
    for step in (2, 1, 3):
        theirs = after(asked[step - 1], found)
        found = attend(place, theirs, all_keys, all_values, heads, piece, tokens)
        parts.append(shift(found, "x", -step))
        if step == 2:
            line = after(line, found)
            line = jnp.broadcast_to(line[None], (4,) + line.shape)
            near = lax.all_to_all(line, "y", 0, 0, tiled=True).reshape(-1, D)
    rows = after(rows, found)
    parts.append(attend(place, rows, all_keys, all_values, heads, piece, tokens))
    near = after(near, parts)
    far = shift(near, "core", 1)

    bests = [part[size].astype(F32) for part in parts]
    best = functools.reduce(jnp.maximum, bests)
    above = jnp.zeros((size, tokens * heads), F32)
    below = jnp.zeros((tokens * heads,), F32)
    for part, top in zip(parts, bests):
        scale = jnp.exp2(top - best)
        above = above + part[:size].astype(F32) * scale[None, :]
        below = below + (part[size + 1].astype(F32) + part[size + 2].astype(F32)) * scale
    context = (above / below[None, :]).astype(BF16).T.reshape(tokens, heads, size)

    order = feature_order(zl, core, heads, size)
    ordered = jnp.dot(
        context.reshape(tokens, heads * size), order, preferred_element_type=F32
    ).astype(BF16)
    mine = jnp.stack([zh]).astype(jnp.int32)
    half = sum_along_x(project(1 - mine, ordered, near, far)).astype(BF16)
    own = after(project(mine, ordered, near, far), half)
    attended = sum_along_x(own) + shift(half, "zh", 1).astype(F32)
    state = resid.astype(F32) + attended
    scaled = (state * gain[None, :]).astype(BF16)

    slots = ctx_count * MOST
    ids = expert_ids.T
    expert = jnp.arange(ctx_count, dtype=jnp.int32)
    named = (ids[:, None, :] == expert[None, :, None]).astype(F32)
    weight = (gate_scores / jnp.sum(gate_scores, axis=1, keepdims=True)).T
    weight = jnp.sum(named * weight[:, None, :], axis=0)
    named = jnp.sum(named, axis=0).astype(BF16)
    token = jnp.arange(tokens, dtype=jnp.int32)
    before = (token[:, None] < token[None, :]).astype(BF16)
    rank = jnp.dot(named, before, preferred_element_type=F32)
    line = jnp.arange(4 * slots, dtype=jnp.int32)
    spread = (line[:, None] // (4 * MOST) == expert[None, :]).astype(BF16)
    weight_high = weight.astype(BF16)
    weight_low = (weight - weight_high.astype(F32)).astype(BF16)
    rank = jnp.where(named > 0, rank, -1.0).astype(BF16)
    tables = jnp.concatenate([rank, weight_high, weight_low], axis=1)
    tables = jnp.dot(spread, tables, preferred_element_type=F32)
    live = tables[:, :tokens] == (line % MOST).astype(F32)[:, None]
    chunk = line // MOST % 4

    def by_chunk(table):
        table = table.astype(BF16)
        zero = jnp.zeros((), BF16)
        return [jnp.where((chunk == c)[:, None], table, zero) for c in range(4)]

    dispatch = jnp.concatenate(by_chunk(live), axis=1)
    combine = jnp.concatenate(
        by_chunk(jnp.where(live, tables[:, tokens : 2 * tokens], 0.0))
        + by_chunk(jnp.where(live, tables[:, 2 * tokens :], 0.0)),
        axis=1,
    )

    lanes = width // 4
    stacked = jnp.concatenate([scaled[:, c * lanes : (c + 1) * lanes] for c in range(4)], axis=0)
    outgoing = jnp.dot(dispatch, stacked, preferred_element_type=F32).astype(BF16)
    outgoing = outgoing.reshape(ctx_count, 4 * MOST, lanes)
    arrived = lax.all_to_all(outgoing, CTX, 0, 0, tiled=True).reshape(4 * slots, lanes)

    units = w_gate_up.shape[3]
    order = swap_order()
    weights = w_gate_up.reshape(width, 2 * units)
    shape = (4, slots // 8, 2 * units + 128)
    half = sum_along_x(gate_up(1 - mine, arrived, order, weights, gain).reshape(shape)).astype(BF16)
    own = after(gate_up(mine, arrived, order, weights, gain).reshape(shape), half)
    part = sum_along_x(own) + shift(half, "zh", 1).astype(F32)
    square = part[:, 2 * units : 2 * units + 1] + part[:, 2 * units + 1 : 2 * units + 2]
    inverse = lax.rsqrt(square / D + EPSILON)
    hidden = (jax.nn.silu(part[:, :units] * inverse) * (part[:, units : 2 * units] * inverse)).astype(
        BF16
    )
    other = shift(hidden, "zh", 1)
    hidden = jnp.where(
        zh == 0, jnp.stack([hidden, other], axis=0), jnp.stack([other, hidden], axis=0)
    )
    hidden = lax.all_gather(hidden, "x", axis=0).reshape(slots, units)
    result = down(hidden, order, w_down[0]).reshape(ctx_count, 4 * MOST, lanes)
    returned = lax.all_to_all(result, CTX, 0, 0, tiled=True).reshape(4 * slots, lanes)
    routed = lax.dot_general(
        combine, returned, (((0,), (0,)), ((), ())), preferred_element_type=F32
    )
    routed = routed[: 4 * tokens] + routed[4 * tokens :]
    routed = jnp.concatenate([routed[c * tokens : (c + 1) * tokens] for c in range(4)], axis=1)
    mixed = (state + routed).astype(BF16)
    return (context, mixed)


def solution(mesh):
    mesh = Mesh(mesh.devices.reshape(4, 8, 2, 2, 4), CTX + EXP)
    in_specs = (
        P(CTX, EXP, None),
        P(CTX, None, None),
        P(CTX, None, None),
        P(CTX, EXP),
        P(EXP),
        P(CTX, None),
        P(CTX, None),
        P(CTX, EXP, None, None),
        P(CTX, None, EXP),
        P(EXP, CTX, None),
    )
    out_specs = (P(CTX, EXP, None), P(CTX, EXP))
    return jax.shard_map(body, mesh=mesh, in_specs=in_specs, out_specs=out_specs, check_vma=False)
```

```python
import functools
import math

import jax
import jax.numpy as jnp
from jax import lax
from jax.experimental import pallas as pl
from jax.experimental.pallas import tpu as pltpu
from jax.sharding import Mesh, PartitionSpec as P

D = 4096
KVH = 2
TOPK = 8
MOST = 10
FLOOR = -1e20
EPSILON = 1e-06
CTX = ("y", "zl", "core")
EXP = ("zh", "x")
SIZES = {"y": 4, "zl": 8, "core": 2, "zh": 2, "x": 4}
F32 = jnp.float32
BF16 = jnp.bfloat16


def shift(value, axis, step):
    count = SIZES[axis]
    return lax.ppermute(value, axis, [(i, (i + step) % count) for i in range(count)])


def partner(value, axis, bit):
    return lax.ppermute(value, axis, [(i, i ^ bit) for i in range(SIZES[axis])])


def after(value, earlier):
    return lax.optimization_barrier((value, earlier))[0]


def double(rows, bit, earlier):
    rows = after(rows, earlier)
    return jnp.concatenate([rows, partner(rows, "zl", bit)], axis=0)


def feature_order(zl, core, heads, size):
    place = lax.broadcasted_iota(jnp.int32, (heads * size, heads * size), 1)
    source = lax.broadcasted_iota(jnp.int32, (heads * size, heads * size), 0)
    inner = place % (2 * heads)
    slot = place // (2 * heads)
    bits = slot % 8
    from_zl = zl ^ (bits // 4 + bits // 2 % 2 * 2 + bits % 2 * 4)
    from_core = jnp.where(slot >= 32, 1 - core, core)
    block = (slot // 8 % 4 * 8 + from_zl) * 2 + from_core
    return (source == inner // 2 * size + block * 2 + inner % 2).astype(BF16)


def project_kernel(side, c_ref, near_ref, far_ref, o_ref):
    half = near_ref.shape[0]
    part = jnp.dot(c_ref[:, :half], near_ref[...], preferred_element_type=F32)
    part = part + jnp.dot(c_ref[:, half:], far_ref[...], preferred_element_type=F32)
    o_ref[0] = part.astype(BF16)


def project(side, ordered, near, far):
    tokens = ordered.shape[0]
    width = D // 8
    return pl.pallas_call(
        project_kernel,
        out_shape=jax.ShapeDtypeStruct((4, tokens, width), BF16),
        grid_spec=pltpu.PrefetchScalarGridSpec(
            num_scalar_prefetch=1,
            grid=(4,),
            in_specs=[
                pl.BlockSpec(ordered.shape, lambda i, side: (0, 0)),
                pl.BlockSpec((near.shape[0], width), lambda i, side: (0, side[0] * 4 + i)),
                pl.BlockSpec((near.shape[0], width), lambda i, side: (0, side[0] * 4 + i)),
            ],
            out_specs=pl.BlockSpec((1, tokens, width), lambda i, side: (i, 0, 0)),
        ),
        compiler_params=pltpu.CompilerParams(vmem_limit_bytes=32 << 20),
        name="project",
    )(side, ordered, near, far)


def sum_along_x(parts):
    return jnp.sum(lax.all_to_all(parts, "x", 0, 0, tiled=True).astype(F32), axis=0)


def swap_order():
    count = 16 * MOST
    into = lax.broadcasted_iota(jnp.int32, (count, count), 0)
    source = lax.broadcasted_iota(jnp.int32, (count, count), 1)
    outer, inner, rank = into // (4 * MOST), into // MOST % 4, into % MOST
    return (source == (inner * 4 + outer) * MOST + rank).astype(BF16)


def gate_up_kernel(side, x_ref, order_ref, w_ref, gain_ref, o_ref, rows_ref):
    step = order_ref.shape[0]
    begin = pl.multiple_of(side[0] * (x_ref.shape[0] // 2), 16)
    quarter = step // 4
    lanes = x_ref.shape[1]
    for b in range(x_ref.shape[0] // step // 2):
        moved = jnp.dot(
            order_ref[...], x_ref[pl.ds(begin + b * step, step), :], preferred_element_type=F32
        ).astype(BF16)
        for c in range(4):
            rows_ref[b * quarter : (b + 1) * quarter, c * lanes : (c + 1) * lanes] = moved[
                c * quarter : (c + 1) * quarter
            ]
    wide = w_ref.shape[1]
    inverse = 1.0 / gain_ref[...]
    step = step // 2
    for b in range(rows_ref.shape[0] // step):
        rows = rows_ref[b * step : (b + 1) * step, :]
        part = jnp.dot(rows, w_ref[...], preferred_element_type=F32)
        o_ref[b * step : (b + 1) * step, 0:wide] = part.astype(BF16)
        plain = rows.astype(F32) * inverse
        square = jnp.sum(plain * plain, axis=1, keepdims=True)
        high = square.astype(BF16).astype(F32)
        lane = lax.broadcasted_iota(jnp.int32, (step, 128), 1)
        extra = jnp.where(lane == 0, high, jnp.where(lane == 1, square - high, 0.0))
        o_ref[b * step : (b + 1) * step, wide : wide + 128] = extra.astype(BF16)


def gate_up(side, arrived, order, weights, gain):
    slots = arrived.shape[0] // 8
    return pl.pallas_call(
        gate_up_kernel,
        out_shape=jax.ShapeDtypeStruct((slots, weights.shape[1] + 128), BF16),
        in_specs=[pl.BlockSpec(memory_space=pltpu.SMEM)] + [pl.BlockSpec(memory_space=pltpu.VMEM)] * 4,
        scratch_shapes=[pltpu.VMEM((slots, weights.shape[0]), BF16)],
        compiler_params=pltpu.CompilerParams(vmem_limit_bytes=48 << 20),
        name="gate_up",
    )(side, arrived, order, weights, gain[None, :])


def down_kernel(h_ref, order_ref, w_ref, o_ref, *, by_x):
    step = order_ref.shape[0]
    quarter = step // 4
    lanes = o_ref.shape[1]
    for a in range(h_ref.shape[0] // step):
        found = jnp.dot(
            h_ref[a * step : (a + 1) * step, :], w_ref[...], preferred_element_type=F32
        )
        for e in range(4):
            b = e // 2 * 8 + a * 2 + e % 2 if by_x else a * 4 + e
            piece = found[e * quarter : (e + 1) * quarter]
            piece = jnp.concatenate(
                [piece[:, c * lanes : (c + 1) * lanes] for c in range(4)], axis=0
            ).astype(BF16)
            o_ref[b * step : (b + 1) * step, :] = jnp.dot(
                order_ref[...], piece, preferred_element_type=F32
            ).astype(BF16)


def down(hidden, order, weights, by_x, name):
    lanes = weights.shape[1] // 4
    return pl.pallas_call(
        functools.partial(down_kernel, by_x=by_x),
        out_shape=jax.ShapeDtypeStruct((hidden.shape[0] * 4, lanes), BF16),
        compiler_params=pltpu.CompilerParams(vmem_limit_bytes=48 << 20),
        name=name,
    )(hidden, order, weights)


def combine_kernel(x_ref, order_ref, w_ref, state_ref, o_ref, rows_ref):
    step = order_ref.shape[0]
    quarter = step // 4
    lanes = x_ref.shape[1]
    for b in range(x_ref.shape[0] // step):
        moved = jnp.dot(
            order_ref[...], x_ref[b * step : (b + 1) * step, :], preferred_element_type=F32
        ).astype(BF16)
        for c in range(4):
            rows_ref[b * quarter : (b + 1) * quarter, c * lanes : (c + 1) * lanes] = moved[
                c * quarter : (c + 1) * quarter
            ]
    routed = lax.dot_general(
        w_ref[...], rows_ref[...], (((0,), (0,)), ((), ())), preferred_element_type=F32
    )
    tokens = state_ref.shape[0]
    o_ref[...] = (state_ref[...] + routed[:tokens] + routed[tokens:]).astype(BF16)


def combine(returned, order, weights, state):
    slots = weights.shape[0]
    return pl.pallas_call(
        combine_kernel,
        out_shape=jax.ShapeDtypeStruct(state.shape, BF16),
        scratch_shapes=[pltpu.VMEM((slots, state.shape[1]), BF16)],
        compiler_params=pltpu.CompilerParams(vmem_limit_bytes=48 << 20),
        name="combine",
    )(returned, order, weights, state)


def attend_kernel(place, q_ref, k_ref, v_ref, o_ref, *, heads, piece, tokens):
    rows = q_ref.shape[0]
    keys = k_ref.shape[0]
    half = keys // 2
    scores = lax.dot_general(
        k_ref[...], q_ref[...], (((1,), (1,)), ((), ())), preferred_element_type=F32
    )
    key = lax.broadcasted_iota(jnp.int32, (keys, rows), 0)
    row = lax.broadcasted_iota(jnp.int32, (keys, rows), 1) + pl.program_id(0) * rows
    core = jnp.where(key >= half, 1 - place[1], place[1])
    block = (key % half) // piece
    key_pos = (block * 2 + core) * tokens + place[2] * piece + key % piece
    row_pos = place[0] + row // heads
    factor = math.log2(math.e) / math.sqrt(q_ref.shape[1])
    masked = jnp.where(key_pos <= row_pos, scores * factor, -1e30)
    best = jnp.max(masked, axis=0, keepdims=True)
    best = jnp.maximum(best, FLOOR).astype(BF16)
    prob = jnp.exp2(masked - best.astype(F32))
    total = jnp.sum(prob, axis=0, keepdims=True)
    high = total.astype(BF16)
    low = (total - high.astype(F32)).astype(BF16)
    summed = lax.dot_general(
        v_ref[...], prob.astype(BF16), (((0,), (0,)), ((), ())), preferred_element_type=F32
    )
    size = v_ref.shape[1]
    o_ref[0:size, :] = summed.astype(BF16)
    line = lax.broadcasted_iota(jnp.int32, (16, rows), 0)
    extra = jnp.where(
        line == 0,
        best.astype(F32),
        jnp.where(line == 1, high.astype(F32), jnp.where(line == 2, low.astype(F32), 0.0)),
    )
    o_ref[size : size + 16, :] = extra.astype(BF16)


def attend(place, rows, keys, values, heads, piece, tokens):
    count, size = rows.shape
    step = 256
    return pl.pallas_call(
        functools.partial(attend_kernel, heads=heads, piece=piece, tokens=tokens),
        out_shape=jax.ShapeDtypeStruct((size + 16, count), BF16),
        grid=(count // step,),
        in_specs=[
            pl.BlockSpec(memory_space=pltpu.SMEM),
            pl.BlockSpec((step, size), lambda i: (i, 0)),
            pl.BlockSpec(keys.shape, lambda i: (0, 0)),
            pl.BlockSpec(values.shape, lambda i: (0, 0)),
        ],
        out_specs=pl.BlockSpec((size + 16, step), lambda i: (0, i)),
        compiler_params=pltpu.CompilerParams(vmem_limit_bytes=48 << 20),
        name="attend",
    )(place, rows, keys, values)


def body(queries, keys, values, resid, gain, expert_ids, gate_scores, w_gate_up, w_down, w_out):
    tokens, heads, size = queries.shape
    y, zl, core = lax.axis_index("y"), lax.axis_index("zl"), lax.axis_index("core")
    zh, x = lax.axis_index("zh"), lax.axis_index("x")
    ctx_place = (y * 8 + zl) * 2 + core
    ctx_count = 64
    width = resid.shape[1]

    piece = tokens // 4
    pair = jnp.stack([keys, values], axis=0)
    pair = lax.dynamic_index_in_dim(pair, zh, 2, keepdims=False)
    pair = lax.dynamic_slice_in_dim(pair, x * piece, piece, 1)
    pair = jnp.broadcast_to(pair[None], (8,) + pair.shape)
    line = w_out.reshape(-1, D)
    line = jnp.concatenate([line, partner(line, "zl", 4)], axis=0)
    pair = first = lax.all_to_all(pair, "zl", 0, 0, tiled=True)
    rows = queries.reshape(tokens * heads, size)
    asked = [shift(rows, "x", step) for step in (1, 2, 3)]
    pair = after(pair, asked)
    pair = jnp.broadcast_to(pair[None], (4,) + pair.shape)
    pair = second = lax.all_to_all(pair, "y", 0, 0, tiled=True)
    line = double(line, 2, first)
    line = double(line, 1, second)
    pair = jnp.stack([pair, shift(pair, "core", 1)], axis=0)
    all_keys = pair[:, :, :, 0].reshape(-1, size)
    all_values = pair[:, :, :, 1].reshape(-1, size)

    place = jnp.stack([ctx_place * tokens, core, x]).astype(jnp.int32)
    parts, found = [], place
    for step in (2, 1, 3):
        theirs = after(asked[step - 1], found)
        found = attend(place, theirs, all_keys, all_values, heads, piece, tokens)
        parts.append(shift(found, "x", -step))
        if step == 2:
            line = after(line, found)
            line = jnp.broadcast_to(line[None], (4,) + line.shape)
            near = lax.all_to_all(line, "y", 0, 0, tiled=True).reshape(-1, D)
    rows = after(rows, found)
    parts.append(attend(place, rows, all_keys, all_values, heads, piece, tokens))
    near = after(near, parts)
    far = shift(near, "core", 1)

    bests = [part[size].astype(F32) for part in parts]
    best = functools.reduce(jnp.maximum, bests)
    above = jnp.zeros((size, tokens * heads), F32)
    below = jnp.zeros((tokens * heads,), F32)
    for part, top in zip(parts, bests):
        scale = jnp.exp2(top - best)
        above = above + part[:size].astype(F32) * scale[None, :]
        below = below + (part[size + 1].astype(F32) + part[size + 2].astype(F32)) * scale
    context = (above / below[None, :]).astype(BF16).T.reshape(tokens, heads, size)

    order = feature_order(zl, core, heads, size)
    ordered = jnp.dot(
        context.reshape(tokens, heads * size), order, preferred_element_type=F32
    ).astype(BF16)
    mine = jnp.stack([zh]).astype(jnp.int32)
    half = sum_along_x(project(1 - mine, ordered, near, far)).astype(BF16)
    own = after(project(mine, ordered, near, far), half)
    attended = sum_along_x(own) + shift(half, "zh", 1).astype(F32)
    state = resid.astype(F32) + attended
    scaled = (state * gain[None, :]).astype(BF16)

    slots = ctx_count * MOST
    ids = after(expert_ids, ordered).T
    expert = jnp.arange(ctx_count, dtype=jnp.int32)
    named = (ids[:, None, :] == expert[None, :, None]).astype(F32)
    weight = (gate_scores / jnp.sum(gate_scores, axis=1, keepdims=True)).T
    weight = jnp.sum(named * weight[:, None, :], axis=0)
    named = jnp.sum(named, axis=0).astype(BF16)
    token = jnp.arange(tokens, dtype=jnp.int32)
    before = (token[:, None] < token[None, :]).astype(BF16)
    rank = jnp.dot(named, before, preferred_element_type=F32)
    line = jnp.arange(slots, dtype=jnp.int32)
    spread = (line[:, None] // MOST == expert[None, :]).astype(BF16)
    weight_high = weight.astype(BF16)
    weight_low = (weight - weight_high.astype(F32)).astype(BF16)
    rank = jnp.where(named > 0, rank, -1.0).astype(BF16)
    tables = jnp.concatenate([rank, weight_high, weight_low], axis=1)
    tables = jnp.dot(spread, tables, preferred_element_type=F32)
    live = tables[:, :tokens] == (line % MOST).astype(F32)[:, None]
    mixing = jnp.where(jnp.concatenate([live, live], axis=1), tables[:, tokens:], 0.0).astype(BF16)

    lanes = width // 4
    order = swap_order()
    outgoing = down(live.astype(BF16), order, scaled, False, "dispatch")
    outgoing = outgoing.reshape(ctx_count, 4 * MOST, lanes)
    arrived = lax.all_to_all(outgoing, CTX, 0, 0, tiled=True).reshape(4 * slots, lanes)

    units = w_gate_up.shape[3]
    weights = w_gate_up.reshape(width, 2 * units)
    shape = (4, slots // 8, 2 * units + 128)
    half = sum_along_x(gate_up(1 - mine, arrived, order, weights, gain).reshape(shape)).astype(BF16)
    own = after(gate_up(mine, arrived, order, weights, gain).reshape(shape), half)
    part = sum_along_x(own) + shift(half, "zh", 1).astype(F32)
    square = part[:, 2 * units : 2 * units + 1] + part[:, 2 * units + 1 : 2 * units + 2]
    inverse = lax.rsqrt(square / D + EPSILON)
    hidden = (jax.nn.silu(part[:, :units] * inverse) * (part[:, units : 2 * units] * inverse)).astype(
        BF16
    )
    other = shift(hidden, "zh", 1)
    hidden = jnp.where(
        zh == 0, jnp.stack([hidden, other], axis=0), jnp.stack([other, hidden], axis=0)
    )
    hidden = lax.all_gather(hidden, "x", axis=0).reshape(slots, units)
    result = down(hidden, order, w_down[0], True, "down").reshape(ctx_count, 4 * MOST, lanes)
    returned = lax.all_to_all(result, CTX, 0, 0, tiled=True).reshape(4 * slots, lanes)
    mixed = combine(returned, order, mixing, state)
    return (context, mixed)


def solution(mesh):
    mesh = Mesh(mesh.devices.reshape(4, 8, 2, 2, 4), CTX + EXP)
    in_specs = (
        P(CTX, EXP, None),
        P(CTX, None, None),
        P(CTX, None, None),
        P(CTX, EXP),
        P(EXP),
        P(CTX, None),
        P(CTX, None),
        P(CTX, EXP, None, None),
        P(CTX, None, EXP),
        P(EXP, CTX, None),
    )
    out_specs = (P(CTX, EXP, None), P(CTX, EXP))
    return jax.shard_map(body, mesh=mesh, in_specs=in_specs, out_specs=out_specs, check_vma=False)
```

```python
import functools
import math

import jax
import jax.numpy as jnp
from jax import lax
from jax.experimental import pallas as pl
from jax.experimental.pallas import tpu as pltpu
from jax.sharding import Mesh, PartitionSpec as P

D = 4096
KVH = 2
TOPK = 8
MOST = 10
FLOOR = -1e20
EPSILON = 1e-06
CTX = ("y", "zl", "core")
EXP = ("zh", "x")
SIZES = {"y": 4, "zl": 8, "core": 2, "zh": 2, "x": 4}
F32 = jnp.float32
BF16 = jnp.bfloat16


def shift(value, axis, step):
    count = SIZES[axis]
    return lax.ppermute(value, axis, [(i, (i + step) % count) for i in range(count)])


def partner(value, axis, bit):
    return lax.ppermute(value, axis, [(i, i ^ bit) for i in range(SIZES[axis])])


def after(value, earlier):
    return lax.optimization_barrier((value, earlier))[0]


def double(rows, bit, earlier):
    found = partner(rows, "zl", bit)
    return jnp.concatenate([after(rows, earlier), found], axis=0)


def feature_order(zl, core, heads, size):
    place = lax.broadcasted_iota(jnp.int32, (heads * size, heads * size), 1)
    source = lax.broadcasted_iota(jnp.int32, (heads * size, heads * size), 0)
    inner = place % (2 * heads)
    slot = place // (2 * heads)
    bits = slot % 8
    from_zl = zl ^ (bits // 4 + bits // 2 % 2 * 2 + bits % 2 * 4)
    from_core = jnp.where(slot >= 32, 1 - core, core)
    block = (slot // 8 % 4 * 8 + from_zl) * 2 + from_core
    return (source == inner // 2 * size + block * 2 + inner % 2).astype(BF16)


def project_kernel(side, c_ref, near_ref, far_ref, o_ref):
    half = near_ref.shape[0]
    part = jnp.dot(c_ref[:, :half], near_ref[...], preferred_element_type=F32)
    part = part + jnp.dot(c_ref[:, half:], far_ref[...], preferred_element_type=F32)
    o_ref[0] = part.astype(BF16)


def project(side, ordered, near, far):
    tokens = ordered.shape[0]
    width = D // 8
    return pl.pallas_call(
        project_kernel,
        out_shape=jax.ShapeDtypeStruct((4, tokens, width), BF16),
        grid_spec=pltpu.PrefetchScalarGridSpec(
            num_scalar_prefetch=1,
            grid=(4,),
            in_specs=[
                pl.BlockSpec(ordered.shape, lambda i, side: (0, 0)),
                pl.BlockSpec((near.shape[0], width), lambda i, side: (0, side[0] * 4 + i)),
                pl.BlockSpec((near.shape[0], width), lambda i, side: (0, side[0] * 4 + i)),
            ],
            out_specs=pl.BlockSpec((1, tokens, width), lambda i, side: (i, 0, 0)),
        ),
        compiler_params=pltpu.CompilerParams(vmem_limit_bytes=32 << 20),
        name="project",
    )(side, ordered, near, far)


def sum_along_x(parts):
    return jnp.sum(lax.all_to_all(parts, "x", 0, 0, tiled=True).astype(F32), axis=0)


def swap_order():
    count = 16 * MOST
    into = lax.broadcasted_iota(jnp.int32, (count, count), 0)
    source = lax.broadcasted_iota(jnp.int32, (count, count), 1)
    outer, inner, rank = into // (4 * MOST), into // MOST % 4, into % MOST
    return (source == (inner * 4 + outer) * MOST + rank).astype(BF16)


def gate_up_kernel(side, x_ref, order_ref, w_ref, gain_ref, o_ref, rows_ref):
    step = order_ref.shape[0]
    begin = pl.multiple_of(side[0] * (x_ref.shape[0] // 2), 16)
    quarter = step // 4
    lanes = x_ref.shape[1]
    for b in range(x_ref.shape[0] // step // 2):
        moved = jnp.dot(
            order_ref[...], x_ref[pl.ds(begin + b * step, step), :], preferred_element_type=F32
        ).astype(BF16)
        for c in range(4):
            rows_ref[b * quarter : (b + 1) * quarter, c * lanes : (c + 1) * lanes] = moved[
                c * quarter : (c + 1) * quarter
            ]
    wide = w_ref.shape[1]
    inverse = 1.0 / gain_ref[...]
    step = step // 2
    for b in range(rows_ref.shape[0] // step):
        rows = rows_ref[b * step : (b + 1) * step, :]
        part = jnp.dot(rows, w_ref[...], preferred_element_type=F32)
        o_ref[b * step : (b + 1) * step, 0:wide] = part.astype(BF16)
        plain = rows.astype(F32) * inverse
        square = jnp.sum(plain * plain, axis=1, keepdims=True)
        high = square.astype(BF16).astype(F32)
        lane = lax.broadcasted_iota(jnp.int32, (step, 128), 1)
        extra = jnp.where(lane == 0, high, jnp.where(lane == 1, square - high, 0.0))
        o_ref[b * step : (b + 1) * step, wide : wide + 128] = extra.astype(BF16)


def gate_up(side, arrived, order, weights, gain):
    slots = arrived.shape[0] // 8
    return pl.pallas_call(
        gate_up_kernel,
        out_shape=jax.ShapeDtypeStruct((slots, weights.shape[1] + 128), BF16),
        in_specs=[pl.BlockSpec(memory_space=pltpu.SMEM)] + [pl.BlockSpec(memory_space=pltpu.VMEM)] * 4,
        scratch_shapes=[pltpu.VMEM((slots, weights.shape[0]), BF16)],
        compiler_params=pltpu.CompilerParams(vmem_limit_bytes=48 << 20),
        name="gate_up",
    )(side, arrived, order, weights, gain[None, :])


def down_kernel(h_ref, order_ref, w_ref, o_ref, *, by_x):
    step = order_ref.shape[0]
    quarter = step // 4
    lanes = o_ref.shape[1]
    for a in range(h_ref.shape[0] // step):
        found = jnp.dot(
            h_ref[a * step : (a + 1) * step, :], w_ref[...], preferred_element_type=F32
        )
        for e in range(4):
            b = e // 2 * 8 + a * 2 + e % 2 if by_x else a * 4 + e
            piece = found[e * quarter : (e + 1) * quarter]
            piece = jnp.concatenate(
                [piece[:, c * lanes : (c + 1) * lanes] for c in range(4)], axis=0
            ).astype(BF16)
            o_ref[b * step : (b + 1) * step, :] = jnp.dot(
                order_ref[...], piece, preferred_element_type=F32
            ).astype(BF16)


def down(hidden, order, weights, by_x, name):
    lanes = weights.shape[1] // 4
    return pl.pallas_call(
        functools.partial(down_kernel, by_x=by_x),
        out_shape=jax.ShapeDtypeStruct((hidden.shape[0] * 4, lanes), BF16),
        compiler_params=pltpu.CompilerParams(vmem_limit_bytes=48 << 20),
        name=name,
    )(hidden, order, weights)


def combine_kernel(x_ref, order_ref, w_ref, state_ref, o_ref, rows_ref):
    step = order_ref.shape[0]
    quarter = step // 4
    lanes = x_ref.shape[1]
    for b in range(x_ref.shape[0] // step):
        moved = jnp.dot(
            order_ref[...], x_ref[b * step : (b + 1) * step, :], preferred_element_type=F32
        ).astype(BF16)
        for c in range(4):
            rows_ref[b * quarter : (b + 1) * quarter, c * lanes : (c + 1) * lanes] = moved[
                c * quarter : (c + 1) * quarter
            ]
    routed = lax.dot_general(
        w_ref[...], rows_ref[...], (((0,), (0,)), ((), ())), preferred_element_type=F32
    )
    tokens = state_ref.shape[0]
    o_ref[...] = (state_ref[...] + routed[:tokens] + routed[tokens:]).astype(BF16)


def combine(returned, order, weights, state):
    slots = weights.shape[0]
    return pl.pallas_call(
        combine_kernel,
        out_shape=jax.ShapeDtypeStruct(state.shape, BF16),
        scratch_shapes=[pltpu.VMEM((slots, state.shape[1]), BF16)],
        compiler_params=pltpu.CompilerParams(vmem_limit_bytes=48 << 20),
        name="combine",
    )(returned, order, weights, state)


def attend_kernel(place, q_ref, k_ref, v_ref, o_ref, *, heads, piece, tokens):
    rows = q_ref.shape[0]
    keys = k_ref.shape[0]
    half = keys // 2
    scores = lax.dot_general(
        k_ref[...], q_ref[...], (((1,), (1,)), ((), ())), preferred_element_type=F32
    )
    blocks = keys // piece
    block = lax.broadcasted_iota(jnp.int32, (blocks, 1, rows), 0)
    core = jnp.where(block >= blocks // 2, 1 - place[1], place[1])
    begin = (block % (blocks // 2) * 2 + core) * tokens + place[2] * piece
    row = lax.broadcasted_iota(jnp.int32, (blocks, 1, rows), 2) + pl.program_id(0) * rows
    ahead = place[0] + row // heads - begin
    inner = lax.broadcasted_iota(jnp.int32, (blocks, piece, rows), 1)
    factor = math.log2(math.e) / math.sqrt(q_ref.shape[1])
    scores = (scores * factor).reshape(blocks, piece, rows)
    masked = jnp.where(inner <= ahead, scores, -1e30).reshape(keys, rows)
    best = jnp.max(masked, axis=0, keepdims=True)
    best = jnp.maximum(best, FLOOR).astype(BF16)
    prob = jnp.exp2(masked - best.astype(F32))
    total = jnp.sum(prob, axis=0, keepdims=True)
    high = total.astype(BF16)
    low = (total - high.astype(F32)).astype(BF16)
    summed = lax.dot_general(
        v_ref[...], prob.astype(BF16), (((0,), (0,)), ((), ())), preferred_element_type=F32
    )
    size = v_ref.shape[1]
    o_ref[0:size, :] = summed.astype(BF16)
    line = lax.broadcasted_iota(jnp.int32, (16, rows), 0)
    extra = jnp.where(
        line == 0,
        best.astype(F32),
        jnp.where(line == 1, high.astype(F32), jnp.where(line == 2, low.astype(F32), 0.0)),
    )
    o_ref[size : size + 16, :] = extra.astype(BF16)


def attend(place, rows, keys, values, heads, piece, tokens):
    count, size = rows.shape
    step = 256
    return pl.pallas_call(
        functools.partial(attend_kernel, heads=heads, piece=piece, tokens=tokens),
        out_shape=jax.ShapeDtypeStruct((size + 16, count), BF16),
        grid=(count // step,),
        in_specs=[
            pl.BlockSpec(memory_space=pltpu.SMEM),
            pl.BlockSpec((step, size), lambda i: (i, 0)),
            pl.BlockSpec(keys.shape, lambda i: (0, 0)),
            pl.BlockSpec(values.shape, lambda i: (0, 0)),
        ],
        out_specs=pl.BlockSpec((size + 16, step), lambda i: (0, i)),
        compiler_params=pltpu.CompilerParams(vmem_limit_bytes=48 << 20),
        name="attend",
    )(place, rows, keys, values)


def body(queries, keys, values, resid, gain, expert_ids, gate_scores, w_gate_up, w_down, w_out):
    tokens, heads, size = queries.shape
    y, zl, core = lax.axis_index("y"), lax.axis_index("zl"), lax.axis_index("core")
    zh, x = lax.axis_index("zh"), lax.axis_index("x")
    ctx_place = (y * 8 + zl) * 2 + core
    ctx_count = 64
    width = resid.shape[1]

    piece = tokens // 4
    pair = jnp.stack([keys, values], axis=0)
    pair = lax.dynamic_index_in_dim(pair, zh, 2, keepdims=False)
    pair = lax.dynamic_slice_in_dim(pair, x * piece, piece, 1)
    pair = jnp.broadcast_to(pair[None], (8,) + pair.shape)
    line = w_out.reshape(-1, D)
    line = jnp.concatenate([line, partner(line, "zl", 4)], axis=0)
    pair = first = lax.all_to_all(pair, "zl", 0, 0, tiled=True)
    rows = queries.reshape(tokens * heads, size)
    beside = partner(rows, "x", 1)
    pair = after(pair, beside)
    pair = jnp.broadcast_to(pair[None], (4,) + pair.shape)
    pair = second = lax.all_to_all(pair, "y", 0, 0, tiled=True)
    across = partner(jnp.concatenate([beside, rows], axis=0), "x", 2)
    line = double(line, 2, first)
    line = double(line, 1, second)
    pair = after(pair, across)
    pair = jnp.stack([pair, shift(pair, "core", 1)], axis=0)
    all_keys = pair[:, :, :, 0].reshape(-1, size)
    all_values = pair[:, :, :, 1].reshape(-1, size)

    place = jnp.stack([ctx_place * tokens, core, x]).astype(jnp.int32)
    line = after(line, all_keys)
    line = jnp.broadcast_to(line[None], (4,) + line.shape)
    near = lax.all_to_all(line, "y", 0, 0, tiled=True).reshape(-1, D)
    parts, found = [], place
    asked = [(1, beside), (3, across[: tokens * heads]), (2, across[tokens * heads :])]
    for bit, theirs in asked:
        theirs = after(theirs, found)
        found = attend(place, theirs, all_keys, all_values, heads, piece, tokens)
        parts.append(partner(found, "x", bit))
    rows = after(rows, found)
    parts.append(attend(place, rows, all_keys, all_values, heads, piece, tokens))
    near = after(near, parts)
    far = shift(near, "core", 1)

    bests = [part[size].astype(F32) for part in parts]
    best = functools.reduce(jnp.maximum, bests)
    above = jnp.zeros((size, tokens * heads), F32)
    below = jnp.zeros((tokens * heads,), F32)
    for part, top in zip(parts, bests):
        scale = jnp.exp2(top - best)
        above = above + part[:size].astype(F32) * scale[None, :]
        below = below + (part[size + 1].astype(F32) + part[size + 2].astype(F32)) * scale
    context = (above / below[None, :]).astype(BF16).T.reshape(tokens, heads, size)

    order = feature_order(zl, core, heads, size)
    ordered = jnp.dot(
        context.reshape(tokens, heads * size), order, preferred_element_type=F32
    ).astype(BF16)
    mine = jnp.stack([zh]).astype(jnp.int32)
    half = sum_along_x(project(1 - mine, ordered, near, far)).astype(BF16)
    own = after(project(mine, ordered, near, far), half)
    attended = sum_along_x(own) + shift(half, "zh", 1).astype(F32)
    state = resid.astype(F32) + attended
    scaled = (state * gain[None, :]).astype(BF16)

    slots = ctx_count * MOST
    ids = after(expert_ids, ordered).T
    expert = jnp.arange(ctx_count, dtype=jnp.int32)
    named = (ids[:, None, :] == expert[None, :, None]).astype(F32)
    weight = (gate_scores / jnp.sum(gate_scores, axis=1, keepdims=True)).T
    weight = jnp.sum(named * weight[:, None, :], axis=0)
    named = jnp.sum(named, axis=0).astype(BF16)
    token = jnp.arange(tokens, dtype=jnp.int32)
    before = (token[:, None] < token[None, :]).astype(BF16)
    rank = jnp.dot(named, before, preferred_element_type=F32)
    line = jnp.arange(slots, dtype=jnp.int32)
    spread = (line[:, None] // MOST == expert[None, :]).astype(BF16)
    weight_high = weight.astype(BF16)
    weight_low = (weight - weight_high.astype(F32)).astype(BF16)
    rank = jnp.where(named > 0, rank, -1.0).astype(BF16)
    tables = jnp.concatenate([rank, weight_high, weight_low], axis=1)
    tables = jnp.dot(spread, tables, preferred_element_type=F32)
    live = tables[:, :tokens] == (line % MOST).astype(F32)[:, None]
    mixing = jnp.where(jnp.concatenate([live, live], axis=1), tables[:, tokens:], 0.0).astype(BF16)

    lanes = width // 4
    order = swap_order()
    outgoing = down(live.astype(BF16), order, scaled, False, "dispatch")
    outgoing = outgoing.reshape(ctx_count, 4 * MOST, lanes)
    arrived = lax.all_to_all(outgoing, CTX, 0, 0, tiled=True).reshape(4 * slots, lanes)

    units = w_gate_up.shape[3]
    weights = w_gate_up.reshape(width, 2 * units)
    shape = (4, slots // 8, 2 * units + 128)
    half = sum_along_x(gate_up(1 - mine, arrived, order, weights, gain).reshape(shape)).astype(BF16)
    own = after(gate_up(mine, arrived, order, weights, gain).reshape(shape), half)
    part = sum_along_x(own) + shift(half, "zh", 1).astype(F32)
    square = part[:, 2 * units : 2 * units + 1] + part[:, 2 * units + 1 : 2 * units + 2]
    inverse = lax.rsqrt(square / D + EPSILON)
    hidden = (jax.nn.silu(part[:, :units] * inverse) * (part[:, units : 2 * units] * inverse)).astype(
        BF16
    )
    other = shift(hidden, "zh", 1)
    hidden = jnp.where(
        zh == 0, jnp.stack([hidden, other], axis=0), jnp.stack([other, hidden], axis=0)
    )
    hidden = lax.all_gather(hidden, "x", axis=0).reshape(slots, units)
    result = down(hidden, order, w_down[0], True, "down").reshape(ctx_count, 4 * MOST, lanes)
    returned = lax.all_to_all(result, CTX, 0, 0, tiled=True).reshape(4 * slots, lanes)
    mixed = combine(returned, order, mixing, state)
    return (context, mixed)


def solution(mesh):
    mesh = Mesh(mesh.devices.reshape(4, 8, 2, 2, 4), CTX + EXP)
    in_specs = (
        P(CTX, EXP, None),
        P(CTX, None, None),
        P(CTX, None, None),
        P(CTX, EXP),
        P(EXP),
        P(CTX, None),
        P(CTX, None),
        P(CTX, EXP, None, None),
        P(CTX, None, EXP),
        P(EXP, CTX, None),
    )
    out_specs = (P(CTX, EXP, None), P(CTX, EXP))
    return jax.shard_map(body, mesh=mesh, in_specs=in_specs, out_specs=out_specs, check_vma=False)
```

```python
import functools
import math

import jax
import jax.numpy as jnp
from jax import lax
from jax.experimental import pallas as pl
from jax.experimental.pallas import tpu as pltpu
from jax.sharding import Mesh, PartitionSpec as P

D = 4096
KVH = 2
TOPK = 8
MOST = 10
FLOOR = -1e20
EPSILON = 1e-06
CTX = ("y", "zl", "core")
EXP = ("zh", "x")
SIZES = {"y": 4, "zl": 8, "core": 2, "zh": 2, "x": 4}
F32 = jnp.float32
BF16 = jnp.bfloat16


def shift(value, axis, step):
    count = SIZES[axis]
    return lax.ppermute(value, axis, [(i, (i + step) % count) for i in range(count)])


def partner(value, axis, bit):
    return lax.ppermute(value, axis, [(i, i ^ bit) for i in range(SIZES[axis])])


def after(value, earlier):
    return lax.optimization_barrier((value, earlier))[0]


def double(rows, bit, earlier):
    rows = after(rows, earlier)
    return jnp.concatenate([rows, partner(rows, "zl", bit)], axis=0)


def feature_order(zl, core, heads, size):
    place = lax.broadcasted_iota(jnp.int32, (heads * size, heads * size), 1)
    source = lax.broadcasted_iota(jnp.int32, (heads * size, heads * size), 0)
    inner = place % (2 * heads)
    slot = place // (2 * heads)
    bits = slot % 8
    from_zl = zl ^ (bits // 4 + bits // 2 % 2 * 2 + bits % 2 * 4)
    from_core = jnp.where(slot >= 32, 1 - core, core)
    block = (slot // 8 % 4 * 8 + from_zl) * 2 + from_core
    return (source == inner // 2 * size + block * 2 + inner % 2).astype(BF16)


def project_kernel(side, c_ref, near_ref, far_ref, o_ref):
    half = near_ref.shape[0]
    part = jnp.dot(c_ref[:, :half], near_ref[...], preferred_element_type=F32)
    part = part + jnp.dot(c_ref[:, half:], far_ref[...], preferred_element_type=F32)
    o_ref[0] = part.astype(BF16)


def project(side, ordered, near, far):
    tokens = ordered.shape[0]
    width = D // 8
    return pl.pallas_call(
        project_kernel,
        out_shape=jax.ShapeDtypeStruct((4, tokens, width), BF16),
        grid_spec=pltpu.PrefetchScalarGridSpec(
            num_scalar_prefetch=1,
            grid=(4,),
            in_specs=[
                pl.BlockSpec(ordered.shape, lambda i, side: (0, 0)),
                pl.BlockSpec((near.shape[0], width), lambda i, side: (0, side[0] * 4 + i)),
                pl.BlockSpec((near.shape[0], width), lambda i, side: (0, side[0] * 4 + i)),
            ],
            out_specs=pl.BlockSpec((1, tokens, width), lambda i, side: (i, 0, 0)),
        ),
        compiler_params=pltpu.CompilerParams(vmem_limit_bytes=32 << 20),
        name="project",
    )(side, ordered, near, far)


def sum_along_x(parts):
    return jnp.sum(lax.all_to_all(parts, "x", 0, 0, tiled=True).astype(F32), axis=0)


def swap_order():
    count = 16 * MOST
    into = lax.broadcasted_iota(jnp.int32, (count, count), 0)
    source = lax.broadcasted_iota(jnp.int32, (count, count), 1)
    outer, inner, rank = into // (4 * MOST), into // MOST % 4, into % MOST
    return (source == (inner * 4 + outer) * MOST + rank).astype(BF16)


def gate_up_kernel(side, x_ref, order_ref, w_ref, gain_ref, o_ref, rows_ref):
    step = order_ref.shape[0]
    begin = pl.multiple_of(side[0] * (x_ref.shape[0] // 2), 16)
    quarter = step // 4
    lanes = x_ref.shape[1]
    for b in range(x_ref.shape[0] // step // 2):
        moved = jnp.dot(
            order_ref[...], x_ref[pl.ds(begin + b * step, step), :], preferred_element_type=F32
        ).astype(BF16)
        for c in range(4):
            rows_ref[b * quarter : (b + 1) * quarter, c * lanes : (c + 1) * lanes] = moved[
                c * quarter : (c + 1) * quarter
            ]
    wide = w_ref.shape[1]
    inverse = 1.0 / gain_ref[...]
    step = step // 2
    for b in range(rows_ref.shape[0] // step):
        rows = rows_ref[b * step : (b + 1) * step, :]
        part = jnp.dot(rows, w_ref[...], preferred_element_type=F32)
        o_ref[b * step : (b + 1) * step, 0:wide] = part.astype(BF16)
        plain = rows.astype(F32) * inverse
        square = jnp.sum(plain * plain, axis=1, keepdims=True)
        high = square.astype(BF16).astype(F32)
        lane = lax.broadcasted_iota(jnp.int32, (step, 128), 1)
        extra = jnp.where(lane == 0, high, jnp.where(lane == 1, square - high, 0.0))
        o_ref[b * step : (b + 1) * step, wide : wide + 128] = extra.astype(BF16)


def gate_up(side, arrived, order, weights, gain):
    slots = arrived.shape[0] // 8
    return pl.pallas_call(
        gate_up_kernel,
        out_shape=jax.ShapeDtypeStruct((slots, weights.shape[1] + 128), BF16),
        in_specs=[pl.BlockSpec(memory_space=pltpu.SMEM)] + [pl.BlockSpec(memory_space=pltpu.VMEM)] * 4,
        scratch_shapes=[pltpu.VMEM((slots, weights.shape[0]), BF16)],
        compiler_params=pltpu.CompilerParams(vmem_limit_bytes=48 << 20),
        name="gate_up",
    )(side, arrived, order, weights, gain[None, :])


def down_kernel(h_ref, order_ref, w_ref, o_ref, *, by_x):
    step = order_ref.shape[0]
    quarter = step // 4
    lanes = o_ref.shape[1]
    for a in range(h_ref.shape[0] // step):
        found = jnp.dot(
            h_ref[a * step : (a + 1) * step, :], w_ref[...], preferred_element_type=F32
        )
        for e in range(4):
            b = e // 2 * 8 + a * 2 + e % 2 if by_x else a * 4 + e
            piece = found[e * quarter : (e + 1) * quarter]
            piece = jnp.concatenate(
                [piece[:, c * lanes : (c + 1) * lanes] for c in range(4)], axis=0
            ).astype(BF16)
            o_ref[b * step : (b + 1) * step, :] = jnp.dot(
                order_ref[...], piece, preferred_element_type=F32
            ).astype(BF16)


def down(hidden, order, weights, by_x, name):
    lanes = weights.shape[1] // 4
    return pl.pallas_call(
        functools.partial(down_kernel, by_x=by_x),
        out_shape=jax.ShapeDtypeStruct((hidden.shape[0] * 4, lanes), BF16),
        compiler_params=pltpu.CompilerParams(vmem_limit_bytes=48 << 20),
        name=name,
    )(hidden, order, weights)


def combine_kernel(x_ref, order_ref, w_ref, state_ref, o_ref, rows_ref):
    step = order_ref.shape[0]
    quarter = step // 4
    lanes = x_ref.shape[1]
    for b in range(x_ref.shape[0] // step):
        moved = jnp.dot(
            order_ref[...], x_ref[b * step : (b + 1) * step, :], preferred_element_type=F32
        ).astype(BF16)
        for c in range(4):
            rows_ref[b * quarter : (b + 1) * quarter, c * lanes : (c + 1) * lanes] = moved[
                c * quarter : (c + 1) * quarter
            ]
    routed = lax.dot_general(
        w_ref[...], rows_ref[...], (((0,), (0,)), ((), ())), preferred_element_type=F32
    )
    tokens = state_ref.shape[0]
    o_ref[...] = (state_ref[...] + routed[:tokens] + routed[tokens:]).astype(BF16)


def combine(returned, order, weights, state):
    slots = weights.shape[0]
    return pl.pallas_call(
        combine_kernel,
        out_shape=jax.ShapeDtypeStruct(state.shape, BF16),
        scratch_shapes=[pltpu.VMEM((slots, state.shape[1]), BF16)],
        compiler_params=pltpu.CompilerParams(vmem_limit_bytes=48 << 20),
        name="combine",
    )(returned, order, weights, state)


def attend_kernel(place, q_ref, k_ref, v_ref, o_ref, *, heads, piece, tokens):
    step = 256
    keys, size = k_ref.shape
    blocks = keys // piece
    factor = math.log2(math.e) / math.sqrt(size)
    block = lax.broadcasted_iota(jnp.int32, (blocks, 1, step), 0)
    core = jnp.where(block >= blocks // 2, 1 - place[1], place[1])
    begin = (block % (blocks // 2) * 2 + core) * tokens + place[2] * piece - place[0]
    row = lax.broadcasted_iota(jnp.int32, (blocks, 1, step), 2) // heads
    inner = lax.broadcasted_iota(jnp.int32, (blocks, piece, step), 1)
    line = lax.broadcasted_iota(jnp.int32, (16, step), 0)
    for i in range(q_ref.shape[0] // step):
        scores = lax.dot_general(
            k_ref[...],
            q_ref[i * step : (i + 1) * step, :],
            (((1,), (1,)), ((), ())),
            preferred_element_type=F32,
        )
        ahead = row + i * step // heads - begin
        scores = (scores * factor).reshape(blocks, piece, step)
        masked = jnp.where(inner <= ahead, scores, -1e30).reshape(keys, step)
        best = jnp.max(masked, axis=0, keepdims=True)
        best = jnp.maximum(best, FLOOR).astype(BF16).astype(F32)
        prob = jnp.exp2(masked - best)
        total = jnp.sum(prob, axis=0, keepdims=True)
        high = total.astype(BF16).astype(F32)
        summed = move(v_ref[...], prob.astype(BF16))
        o_ref[0:size, i * step : (i + 1) * step] = summed.astype(BF16)
        extra = jnp.where(line == 1, high, jnp.where(line == 2, total - high, 0.0))
        extra = jnp.where(line == 0, best, extra)
        o_ref[size : size + 16, i * step : (i + 1) * step] = extra.astype(BF16)


def move(matrix, rows):
    return lax.dot_general(matrix, rows, (((0,), (0,)), ((), ())), preferred_element_type=F32)


def attend(place, rows, keys, values, heads, piece, tokens):
    count, size = rows.shape
    return pl.pallas_call(
        functools.partial(attend_kernel, heads=heads, piece=piece, tokens=tokens),
        out_shape=jax.ShapeDtypeStruct((size + 16, count), BF16),
        in_specs=[pl.BlockSpec(memory_space=pltpu.SMEM)] + [pl.BlockSpec(memory_space=pltpu.VMEM)] * 3,
        compiler_params=pltpu.CompilerParams(vmem_limit_bytes=48 << 20),
        name="attend",
    )(place, rows, keys, values)


def body(queries, keys, values, resid, gain, expert_ids, gate_scores, w_gate_up, w_down, w_out):
    tokens, heads, size = queries.shape
    y, zl, core = lax.axis_index("y"), lax.axis_index("zl"), lax.axis_index("core")
    zh, x = lax.axis_index("zh"), lax.axis_index("x")
    ctx_place = (y * 8 + zl) * 2 + core
    ctx_count = 64
    width = resid.shape[1]

    piece = tokens // 4
    pair = jnp.stack([keys, values], axis=0)
    pair = lax.dynamic_index_in_dim(pair, zh, 2, keepdims=False)
    pair = lax.dynamic_slice_in_dim(pair, x * piece, piece, 1)
    pair = jnp.broadcast_to(pair[None], (8,) + pair.shape)
    line = w_out.reshape(-1, D)
    line = jnp.concatenate([line, partner(line, "zl", 4)], axis=0)
    pair = first = lax.all_to_all(pair, "zl", 0, 0, tiled=True)
    rows = queries.reshape(tokens * heads, size)
    beside = partner(rows, "x", 1)
    pair = after(pair, beside)
    pair = jnp.broadcast_to(pair[None], (4,) + pair.shape)
    pair = second = lax.all_to_all(pair, "y", 0, 0, tiled=True)
    across = partner(jnp.concatenate([beside, after(rows, first)], axis=0), "x", 2)
    line = double(line, 2, first)
    found = partner(line, "zl", 1)
    line = jnp.concatenate([after(line, second), found], axis=0)
    pair = after(pair, across)
    pair = jnp.stack([pair, shift(pair, "core", 1)], axis=0)
    all_keys = pair[:, :, :, 0].reshape(-1, size)
    all_values = pair[:, :, :, 1].reshape(-1, size)

    place = jnp.stack([ctx_place * tokens, core, x]).astype(jnp.int32)
    line = after(line, all_keys)
    line = jnp.broadcast_to(line[None], (4,) + line.shape)
    near = lax.all_to_all(line, "y", 0, 0, tiled=True).reshape(-1, D)
    parts, found = [], place
    asked = [(1, beside), (3, across[: tokens * heads]), (2, across[tokens * heads :])]
    for bit, theirs in asked:
        theirs = after(theirs, found)
        found = attend(place, theirs, all_keys, all_values, heads, piece, tokens)
        parts.append(partner(found, "x", bit))
    rows = after(rows, found)
    parts.append(attend(place, rows, all_keys, all_values, heads, piece, tokens))
    near = after(near, parts)
    far = shift(near, "core", 1)

    bests = [part[size].astype(F32) for part in parts]
    best = functools.reduce(jnp.maximum, bests)
    above = jnp.zeros((size, tokens * heads), F32)
    below = jnp.zeros((tokens * heads,), F32)
    for part, top in zip(parts, bests):
        scale = jnp.exp2(top - best)
        above = above + part[:size].astype(F32) * scale[None, :]
        below = below + (part[size + 1].astype(F32) + part[size + 2].astype(F32)) * scale
    context = (above / below[None, :]).astype(BF16).T.reshape(tokens, heads, size)

    order = feature_order(zl, core, heads, size)
    ordered = jnp.dot(
        context.reshape(tokens, heads * size), order, preferred_element_type=F32
    ).astype(BF16)
    mine = jnp.stack([zh]).astype(jnp.int32)
    half = sum_along_x(project(1 - mine, ordered, near, far)).astype(BF16)
    own = after(project(mine, ordered, near, far), half)
    attended = sum_along_x(own) + shift(half, "zh", 1).astype(F32)
    state = resid.astype(F32) + attended
    scaled = (state * gain[None, :]).astype(BF16)

    slots = ctx_count * MOST
    ids = after(expert_ids, ordered).T
    expert = jnp.arange(ctx_count, dtype=jnp.int32)
    named = (ids[:, None, :] == expert[None, :, None]).astype(F32)
    weight = (gate_scores / jnp.sum(gate_scores, axis=1, keepdims=True)).T
    weight = jnp.sum(named * weight[:, None, :], axis=0)
    named = jnp.sum(named, axis=0).astype(BF16)
    token = jnp.arange(tokens, dtype=jnp.int32)
    before = (token[:, None] < token[None, :]).astype(BF16)
    rank = jnp.dot(named, before, preferred_element_type=F32)
    line = jnp.arange(slots, dtype=jnp.int32)
    spread = (line[:, None] // MOST == expert[None, :]).astype(BF16)
    weight_high = weight.astype(BF16)
    weight_low = (weight - weight_high.astype(F32)).astype(BF16)
    rank = jnp.where(named > 0, rank, -1.0).astype(BF16)
    tables = jnp.concatenate([rank, weight_high, weight_low], axis=1)
    tables = jnp.dot(spread, tables, preferred_element_type=F32)
    live = tables[:, :tokens] == (line % MOST).astype(F32)[:, None]
    mixing = jnp.where(jnp.concatenate([live, live], axis=1), tables[:, tokens:], 0.0).astype(BF16)

    lanes = width // 4
    order = swap_order()
    outgoing = down(live.astype(BF16), order, scaled, False, "dispatch")
    outgoing = outgoing.reshape(ctx_count, 4 * MOST, lanes)
    arrived = lax.all_to_all(outgoing, CTX, 0, 0, tiled=True).reshape(4 * slots, lanes)

    units = w_gate_up.shape[3]
    weights = w_gate_up.reshape(width, 2 * units)
    shape = (4, slots // 8, 2 * units + 128)
    half = sum_along_x(gate_up(1 - mine, arrived, order, weights, gain).reshape(shape)).astype(BF16)
    own = after(gate_up(mine, arrived, order, weights, gain).reshape(shape), half)
    part = sum_along_x(own) + shift(half, "zh", 1).astype(F32)
    square = part[:, 2 * units : 2 * units + 1] + part[:, 2 * units + 1 : 2 * units + 2]
    inverse = lax.rsqrt(square / D + EPSILON)
    hidden = (jax.nn.silu(part[:, :units] * inverse) * (part[:, units : 2 * units] * inverse)).astype(
        BF16
    )
    other = shift(hidden, "zh", 1)
    hidden = jnp.where(
        zh == 0, jnp.stack([hidden, other], axis=0), jnp.stack([other, hidden], axis=0)
    )
    hidden = lax.all_gather(hidden, "x", axis=0).reshape(slots, units)
    result = down(hidden, order, w_down[0], True, "down").reshape(ctx_count, 4 * MOST, lanes)
    returned = lax.all_to_all(result, CTX, 0, 0, tiled=True).reshape(4 * slots, lanes)
    mixed = combine(returned, order, mixing, state)
    return (context, mixed)


def solution(mesh):
    mesh = Mesh(mesh.devices.reshape(4, 8, 2, 2, 4), CTX + EXP)
    in_specs = (
        P(CTX, EXP, None),
        P(CTX, None, None),
        P(CTX, None, None),
        P(CTX, EXP),
        P(EXP),
        P(CTX, None),
        P(CTX, None),
        P(CTX, EXP, None, None),
        P(CTX, None, EXP),
        P(EXP, CTX, None),
    )
    out_specs = (P(CTX, EXP, None), P(CTX, EXP))
    return jax.shard_map(body, mesh=mesh, in_specs=in_specs, out_specs=out_specs, check_vma=False)
```

```python
import functools
import math

import jax
import jax.numpy as jnp
from jax import lax
from jax.experimental import pallas as pl
from jax.experimental.pallas import tpu as pltpu
from jax.sharding import Mesh, PartitionSpec as P

D = 4096
KVH = 2
TOPK = 8
MOST = 10
FLOOR = -1e20
EPSILON = 1e-06
CTX = ("y", "zl", "core")
EXP = ("zh", "x")
SIZES = {"y": 4, "zl": 8, "core": 2, "zh": 2, "x": 4}
F32 = jnp.float32
BF16 = jnp.bfloat16


def shift(value, axis, step):
    count = SIZES[axis]
    return lax.ppermute(value, axis, [(i, (i + step) % count) for i in range(count)])


def partner(value, axis, bit):
    return lax.ppermute(value, axis, [(i, i ^ bit) for i in range(SIZES[axis])])


def after(value, earlier):
    return lax.optimization_barrier((value, earlier))[0]


def double(rows, bit, earlier):
    rows = after(rows, earlier)
    return jnp.concatenate([rows, partner(rows, "zl", bit)], axis=0)


def feature_order(zl, core, heads, size):
    place = lax.broadcasted_iota(jnp.int32, (heads * size, heads * size), 1)
    source = lax.broadcasted_iota(jnp.int32, (heads * size, heads * size), 0)
    inner = place % (2 * heads)
    slot = place // (2 * heads)
    bits = slot % 8
    from_zl = zl ^ (bits // 4 + bits // 2 % 2 * 2 + bits % 2 * 4)
    from_core = jnp.where(slot >= 32, 1 - core, core)
    block = (slot // 8 % 4 * 8 + from_zl) * 2 + from_core
    return (source == inner // 2 * size + block * 2 + inner % 2).astype(BF16)


def project_kernel(side, c_ref, near_ref, far_ref, o_ref):
    half = near_ref.shape[0]
    width = o_ref.shape[2]
    part = jnp.dot(c_ref[:, :half], near_ref[...], preferred_element_type=F32)
    part = part + jnp.dot(c_ref[:, half:], far_ref[...], preferred_element_type=F32)
    for i in range(o_ref.shape[0]):
        o_ref[i] = part[:, i * width : (i + 1) * width].astype(BF16)


def project(side, ordered, near, far):
    tokens = ordered.shape[0]
    width = D // 8
    return pl.pallas_call(
        project_kernel,
        out_shape=jax.ShapeDtypeStruct((4, tokens, width), BF16),
        grid_spec=pltpu.PrefetchScalarGridSpec(
            num_scalar_prefetch=1,
            grid=(2,),
            in_specs=[
                pl.BlockSpec(ordered.shape, lambda i, side: (0, 0)),
                pl.BlockSpec((near.shape[0], 2 * width), lambda i, side: (0, side[0] * 2 + i)),
                pl.BlockSpec((near.shape[0], 2 * width), lambda i, side: (0, side[0] * 2 + i)),
            ],
            out_specs=pl.BlockSpec((2, tokens, width), lambda i, side: (i, 0, 0)),
        ),
        compiler_params=pltpu.CompilerParams(vmem_limit_bytes=32 << 20),
        name="project",
    )(side, ordered, near, far)


def sum_along_x(parts):
    return jnp.sum(lax.all_to_all(parts, "x", 0, 0, tiled=True).astype(F32), axis=0)


def swap_order():
    count = 16 * MOST
    into = lax.broadcasted_iota(jnp.int32, (count, count), 0)
    source = lax.broadcasted_iota(jnp.int32, (count, count), 1)
    outer, inner, rank = into // (4 * MOST), into // MOST % 4, into % MOST
    return (source == (inner * 4 + outer) * MOST + rank).astype(BF16)


def gate_up_kernel(side, x_ref, order_ref, w_ref, gain_ref, o_ref, rows_ref):
    step = order_ref.shape[0]
    begin = pl.multiple_of(side[0] * (x_ref.shape[0] // 2), 16)
    quarter = step // 4
    lanes = x_ref.shape[1]
    for b in range(x_ref.shape[0] // step // 2):
        moved = jnp.dot(
            order_ref[...], x_ref[pl.ds(begin + b * step, step), :], preferred_element_type=F32
        ).astype(BF16)
        for c in range(4):
            rows_ref[b * quarter : (b + 1) * quarter, c * lanes : (c + 1) * lanes] = moved[
                c * quarter : (c + 1) * quarter
            ]
    wide = w_ref.shape[1]
    inverse = 1.0 / gain_ref[...]
    step = step // 2
    for b in range(rows_ref.shape[0] // step):
        rows = rows_ref[b * step : (b + 1) * step, :]
        part = jnp.dot(rows, w_ref[...], preferred_element_type=F32)
        o_ref[b * step : (b + 1) * step, 0:wide] = part.astype(BF16)
        plain = rows.astype(F32) * inverse
        square = jnp.sum(plain * plain, axis=1, keepdims=True)
        high = square.astype(BF16).astype(F32)
        lane = lax.broadcasted_iota(jnp.int32, (step, 128), 1)
        extra = jnp.where(lane == 0, high, jnp.where(lane == 1, square - high, 0.0))
        o_ref[b * step : (b + 1) * step, wide : wide + 128] = extra.astype(BF16)


def gate_up(side, arrived, order, weights, gain):
    slots = arrived.shape[0] // 8
    return pl.pallas_call(
        gate_up_kernel,
        out_shape=jax.ShapeDtypeStruct((slots, weights.shape[1] + 128), BF16),
        in_specs=[pl.BlockSpec(memory_space=pltpu.SMEM)] + [pl.BlockSpec(memory_space=pltpu.VMEM)] * 4,
        scratch_shapes=[pltpu.VMEM((slots, weights.shape[0]), BF16)],
        compiler_params=pltpu.CompilerParams(vmem_limit_bytes=48 << 20),
        name="gate_up",
    )(side, arrived, order, weights, gain[None, :])


def down_kernel(h_ref, order_ref, w_ref, o_ref, *, by_x):
    step = order_ref.shape[0]
    quarter = step // 4
    lanes = o_ref.shape[1]
    for a in range(h_ref.shape[0] // step):
        found = jnp.dot(
            h_ref[a * step : (a + 1) * step, :], w_ref[...], preferred_element_type=F32
        )
        for e in range(4):
            b = e // 2 * 8 + a * 2 + e % 2 if by_x else a * 4 + e
            piece = found[e * quarter : (e + 1) * quarter]
            piece = jnp.concatenate(
                [piece[:, c * lanes : (c + 1) * lanes] for c in range(4)], axis=0
            ).astype(BF16)
            o_ref[b * step : (b + 1) * step, :] = jnp.dot(
                order_ref[...], piece, preferred_element_type=F32
            ).astype(BF16)


def down(hidden, order, weights, by_x, name):
    lanes = weights.shape[1] // 4
    return pl.pallas_call(
        functools.partial(down_kernel, by_x=by_x),
        out_shape=jax.ShapeDtypeStruct((hidden.shape[0] * 4, lanes), BF16),
        compiler_params=pltpu.CompilerParams(vmem_limit_bytes=48 << 20),
        name=name,
    )(hidden, order, weights)


def combine_kernel(x_ref, order_ref, w_ref, state_ref, o_ref, rows_ref):
    step = order_ref.shape[0]
    quarter = step // 4
    lanes = x_ref.shape[1]
    for b in range(x_ref.shape[0] // step):
        moved = jnp.dot(
            order_ref[...], x_ref[b * step : (b + 1) * step, :], preferred_element_type=F32
        ).astype(BF16)
        for c in range(4):
            rows_ref[b * quarter : (b + 1) * quarter, c * lanes : (c + 1) * lanes] = moved[
                c * quarter : (c + 1) * quarter
            ]
    routed = lax.dot_general(
        w_ref[...], rows_ref[...], (((0,), (0,)), ((), ())), preferred_element_type=F32
    )
    tokens = state_ref.shape[0]
    o_ref[...] = (state_ref[...] + routed[:tokens] + routed[tokens:]).astype(BF16)


def combine(returned, order, weights, state):
    slots = weights.shape[0]
    return pl.pallas_call(
        combine_kernel,
        out_shape=jax.ShapeDtypeStruct(state.shape, BF16),
        scratch_shapes=[pltpu.VMEM((slots, state.shape[1]), BF16)],
        compiler_params=pltpu.CompilerParams(vmem_limit_bytes=48 << 20),
        name="combine",
    )(returned, order, weights, state)


def attend_kernel(place, q_ref, k_ref, v_ref, o_ref, *, heads, piece, tokens):
    step = 512
    keys, size = k_ref.shape
    blocks = keys // piece
    factor = math.log2(math.e) / math.sqrt(size)
    block = lax.broadcasted_iota(jnp.int32, (blocks, 1, step), 0)
    core = jnp.where(block >= blocks // 2, 1 - place[1], place[1])
    begin = (block % (blocks // 2) * 2 + core) * tokens + place[2] * piece - place[0]
    row = lax.broadcasted_iota(jnp.int32, (blocks, 1, step), 2) // heads
    inner = lax.broadcasted_iota(jnp.int32, (blocks, piece, step), 1)
    line = lax.broadcasted_iota(jnp.int32, (16, step), 0)
    for i in range(q_ref.shape[0] // step):
        scores = lax.dot_general(
            k_ref[...],
            q_ref[i * step : (i + 1) * step, :],
            (((1,), (1,)), ((), ())),
            preferred_element_type=F32,
        )
        ahead = row + i * step // heads - begin
        scores = (scores * factor).reshape(blocks, piece, step)
        masked = jnp.where(inner <= ahead, scores, -1e30).reshape(keys, step)
        best = jnp.max(masked, axis=0, keepdims=True)
        best = jnp.maximum(best, FLOOR).astype(BF16).astype(F32)
        prob = jnp.exp2(masked - best)
        total = jnp.sum(prob, axis=0, keepdims=True)
        high = total.astype(BF16).astype(F32)
        summed = move(v_ref[...], prob.astype(BF16))
        o_ref[0:size, i * step : (i + 1) * step] = summed.astype(BF16)
        extra = jnp.where(line == 1, high, jnp.where(line == 2, total - high, 0.0))
        extra = jnp.where(line == 0, best, extra)
        o_ref[size : size + 16, i * step : (i + 1) * step] = extra.astype(BF16)


def move(matrix, rows):
    return lax.dot_general(matrix, rows, (((0,), (0,)), ((), ())), preferred_element_type=F32)


def attend(place, rows, keys, values, heads, piece, tokens):
    count, size = rows.shape
    return pl.pallas_call(
        functools.partial(attend_kernel, heads=heads, piece=piece, tokens=tokens),
        out_shape=jax.ShapeDtypeStruct((size + 16, count), BF16),
        in_specs=[pl.BlockSpec(memory_space=pltpu.SMEM)] + [pl.BlockSpec(memory_space=pltpu.VMEM)] * 3,
        compiler_params=pltpu.CompilerParams(vmem_limit_bytes=48 << 20),
        name="attend",
    )(place, rows, keys, values)


def body(queries, keys, values, resid, gain, expert_ids, gate_scores, w_gate_up, w_down, w_out):
    tokens, heads, size = queries.shape
    y, zl, core = lax.axis_index("y"), lax.axis_index("zl"), lax.axis_index("core")
    zh, x = lax.axis_index("zh"), lax.axis_index("x")
    ctx_place = (y * 8 + zl) * 2 + core
    ctx_count = 64
    width = resid.shape[1]

    piece = tokens // 4
    pair = jnp.stack([keys, values], axis=0)
    pair = lax.dynamic_index_in_dim(pair, zh, 2, keepdims=False)
    pair = lax.dynamic_slice_in_dim(pair, x * piece, piece, 1)
    pair = jnp.broadcast_to(pair[None], (8,) + pair.shape)
    line = w_out.reshape(-1, D)
    line = jnp.concatenate([line, partner(line, "zl", 4)], axis=0)
    pair = first = lax.all_to_all(pair, "zl", 0, 0, tiled=True)
    rows = queries.reshape(tokens * heads, size)
    beside = partner(rows, "x", 1)
    pair = after(pair, beside)
    pair = jnp.broadcast_to(pair[None], (4,) + pair.shape)
    pair = second = lax.all_to_all(pair, "y", 0, 0, tiled=True)
    across = partner(jnp.concatenate([beside, after(rows, first)], axis=0), "x", 2)
    line = double(line, 2, first)
    found = partner(line, "zl", 1)
    line = jnp.concatenate([after(line, second), found], axis=0)
    pair = after(pair, across)
    pair = jnp.stack([pair, shift(pair, "core", 1)], axis=0)
    all_keys = pair[:, :, :, 0].reshape(-1, size)
    all_values = pair[:, :, :, 1].reshape(-1, size)

    place = jnp.stack([ctx_place * tokens, core, x]).astype(jnp.int32)
    line = after(line, all_keys)
    line = jnp.broadcast_to(line[None], (4,) + line.shape)
    near = lax.all_to_all(line, "y", 0, 0, tiled=True).reshape(-1, D)
    parts, found = [], place
    asked = [(1, beside), (3, across[: tokens * heads]), (2, across[tokens * heads :])]
    for bit, theirs in asked:
        theirs = after(theirs, found)
        found = attend(place, theirs, all_keys, all_values, heads, piece, tokens)
        parts.append(partner(found, "x", bit))
    rows = after(rows, found)
    parts.append(attend(place, rows, all_keys, all_values, heads, piece, tokens))
    near = after(near, parts)
    far = shift(near, "core", 1)

    bests = [part[size].astype(F32) for part in parts]
    best = functools.reduce(jnp.maximum, bests)
    above = jnp.zeros((size, tokens * heads), F32)
    below = jnp.zeros((tokens * heads,), F32)
    for part, top in zip(parts, bests):
        scale = jnp.exp2(top - best)
        above = above + part[:size].astype(F32) * scale[None, :]
        below = below + (part[size + 1].astype(F32) + part[size + 2].astype(F32)) * scale
    context = (above / below[None, :]).astype(BF16).T.reshape(tokens, heads, size)

    order = feature_order(zl, core, heads, size)
    ordered = jnp.dot(
        context.reshape(tokens, heads * size), order, preferred_element_type=F32
    ).astype(BF16)
    mine = jnp.stack([zh]).astype(jnp.int32)
    half = sum_along_x(project(1 - mine, ordered, near, far)).astype(BF16)
    own = after(project(mine, ordered, near, far), half)
    attended = sum_along_x(own) + shift(half, "zh", 1).astype(F32)
    state = resid.astype(F32) + attended
    scaled = (state * gain[None, :]).astype(BF16)

    slots = ctx_count * MOST
    ids = after(expert_ids, ordered).T
    expert = jnp.arange(ctx_count, dtype=jnp.int32)
    named = (ids[:, None, :] == expert[None, :, None]).astype(F32)
    weight = (gate_scores / jnp.sum(gate_scores, axis=1, keepdims=True)).T
    weight = jnp.sum(named * weight[:, None, :], axis=0)
    named = jnp.sum(named, axis=0).astype(BF16)
    token = jnp.arange(tokens, dtype=jnp.int32)
    before = (token[:, None] < token[None, :]).astype(BF16)
    rank = jnp.dot(named, before, preferred_element_type=F32)
    line = jnp.arange(slots, dtype=jnp.int32)
    spread = (line[:, None] // MOST == expert[None, :]).astype(BF16)
    weight_high = weight.astype(BF16)
    weight_low = (weight - weight_high.astype(F32)).astype(BF16)
    rank = jnp.where(named > 0, rank, -1.0).astype(BF16)
    tables = jnp.concatenate([rank, weight_high, weight_low], axis=1)
    tables = jnp.dot(spread, tables, preferred_element_type=F32)
    live = tables[:, :tokens] == (line % MOST).astype(F32)[:, None]
    mixing = jnp.where(jnp.concatenate([live, live], axis=1), tables[:, tokens:], 0.0).astype(BF16)

    lanes = width // 4
    order = swap_order()
    outgoing = down(live.astype(BF16), order, scaled, False, "dispatch")
    outgoing = outgoing.reshape(ctx_count, 4 * MOST, lanes)
    arrived = lax.all_to_all(outgoing, CTX, 0, 0, tiled=True).reshape(4 * slots, lanes)

    units = w_gate_up.shape[3]
    weights = w_gate_up.reshape(width, 2 * units)
    shape = (4, slots // 8, 2 * units + 128)
    half = sum_along_x(gate_up(1 - mine, arrived, order, weights, gain).reshape(shape)).astype(BF16)
    own = after(gate_up(mine, arrived, order, weights, gain).reshape(shape), half)
    part = sum_along_x(own) + shift(half, "zh", 1).astype(F32)
    square = part[:, 2 * units : 2 * units + 1] + part[:, 2 * units + 1 : 2 * units + 2]
    inverse = lax.rsqrt(square / D + EPSILON)
    hidden = (jax.nn.silu(part[:, :units] * inverse) * (part[:, units : 2 * units] * inverse)).astype(
        BF16
    )
    other = shift(hidden, "zh", 1)
    hidden = jnp.where(
        zh == 0, jnp.stack([hidden, other], axis=0), jnp.stack([other, hidden], axis=0)
    )
    hidden = lax.all_gather(hidden, "x", axis=0).reshape(slots, units)
    result = down(hidden, order, w_down[0], True, "down").reshape(ctx_count, 4 * MOST, lanes)
    returned = lax.all_to_all(result, CTX, 0, 0, tiled=True).reshape(4 * slots, lanes)
    mixed = combine(returned, order, mixing, state)
    return (context, mixed)


def solution(mesh):
    mesh = Mesh(mesh.devices.reshape(4, 8, 2, 2, 4), CTX + EXP)
    in_specs = (
        P(CTX, EXP, None),
        P(CTX, None, None),
        P(CTX, None, None),
        P(CTX, EXP),
        P(EXP),
        P(CTX, None),
        P(CTX, None),
        P(CTX, EXP, None, None),
        P(CTX, None, EXP),
        P(EXP, CTX, None),
    )
    out_specs = (P(CTX, EXP, None), P(CTX, EXP))
    return jax.shard_map(body, mesh=mesh, in_specs=in_specs, out_specs=out_specs, check_vma=False)
```

```python
import functools
import math

import jax
import jax.numpy as jnp
from jax import lax
from jax.experimental import pallas as pl
from jax.experimental.pallas import tpu as pltpu
from jax.sharding import Mesh, PartitionSpec as P

D = 4096
KVH = 2
TOPK = 8
MOST = 10
FLOOR = -1e20
EPSILON = 1e-06
CTX = ("y", "zl", "core")
EXP = ("zh", "x")
SIZES = {"y": 4, "zl": 8, "core": 2, "zh": 2, "x": 4}
F32 = jnp.float32
BF16 = jnp.bfloat16


def shift(value, axis, step):
    count = SIZES[axis]
    return lax.ppermute(value, axis, [(i, (i + step) % count) for i in range(count)])


def partner(value, axis, bit):
    return lax.ppermute(value, axis, [(i, i ^ bit) for i in range(SIZES[axis])])


def after(value, earlier):
    return lax.optimization_barrier((value, earlier))[0]


def double(rows, bit, earlier):
    rows = after(rows, earlier)
    return jnp.concatenate([rows, partner(rows, "zl", bit)], axis=0)


def feature_order(zl, core, heads, size):
    place = lax.broadcasted_iota(jnp.int32, (heads * size, heads * size), 1)
    source = lax.broadcasted_iota(jnp.int32, (heads * size, heads * size), 0)
    inner = place % (2 * heads)
    slot = place // (2 * heads)
    bits = slot % 8
    from_zl = zl ^ (bits // 4 + bits // 2 % 2 * 2 + bits % 2 * 4)
    from_core = jnp.where(slot >= 32, 1 - core, core)
    block = (slot // 8 % 4 * 8 + from_zl) * 2 + from_core
    return (source == inner // 2 * size + block * 2 + inner % 2).astype(BF16)


def project_kernel(side, c_ref, near_ref, far_ref, o_ref):
    half = near_ref.shape[0]
    width = o_ref.shape[2]
    part = jnp.dot(c_ref[:, :half], near_ref[...], preferred_element_type=F32)
    part = part + jnp.dot(c_ref[:, half:], far_ref[...], preferred_element_type=F32)
    for i in range(o_ref.shape[0]):
        o_ref[i] = part[:, i * width : (i + 1) * width].astype(BF16)


def project(side, ordered, near, far):
    tokens = ordered.shape[0]
    width = D // 8
    return pl.pallas_call(
        project_kernel,
        out_shape=jax.ShapeDtypeStruct((4, tokens, width), BF16),
        grid_spec=pltpu.PrefetchScalarGridSpec(
            num_scalar_prefetch=1,
            grid=(2,),
            in_specs=[
                pl.BlockSpec(ordered.shape, lambda i, side: (0, 0)),
                pl.BlockSpec((near.shape[0], 2 * width), lambda i, side: (0, side[0] * 2 + i)),
                pl.BlockSpec((near.shape[0], 2 * width), lambda i, side: (0, side[0] * 2 + i)),
            ],
            out_specs=pl.BlockSpec((2, tokens, width), lambda i, side: (i, 0, 0)),
        ),
        compiler_params=pltpu.CompilerParams(vmem_limit_bytes=32 << 20),
        name="project",
    )(side, ordered, near, far)


def sum_along_x(parts):
    return jnp.sum(lax.all_to_all(parts, "x", 0, 0, tiled=True).astype(F32), axis=0)


def swap_order():
    count = 16 * MOST
    into = lax.broadcasted_iota(jnp.int32, (count, count), 0)
    source = lax.broadcasted_iota(jnp.int32, (count, count), 1)
    outer, inner, rank = into // (4 * MOST), into // MOST % 4, into % MOST
    return (source == (inner * 4 + outer) * MOST + rank).astype(BF16)


def gate_up_kernel(side, x_ref, order_ref, w_ref, gain_ref, o_ref, rows_ref):
    step = order_ref.shape[0]
    begin = pl.multiple_of(side[0] * (x_ref.shape[0] // 2), 16)
    quarter = step // 4
    lanes = x_ref.shape[1]
    for b in range(x_ref.shape[0] // step // 2):
        moved = jnp.dot(
            order_ref[...], x_ref[pl.ds(begin + b * step, step), :], preferred_element_type=F32
        ).astype(BF16)
        for c in range(4):
            rows_ref[b * quarter : (b + 1) * quarter, c * lanes : (c + 1) * lanes] = moved[
                c * quarter : (c + 1) * quarter
            ]
    wide = w_ref.shape[1]
    inverse = 1.0 / gain_ref[...]
    step = step // 2
    for b in range(rows_ref.shape[0] // step):
        rows = rows_ref[b * step : (b + 1) * step, :]
        part = jnp.dot(rows, w_ref[...], preferred_element_type=F32)
        o_ref[b * step : (b + 1) * step, 0:wide] = part.astype(BF16)
        plain = rows.astype(F32) * inverse
        square = jnp.sum(plain * plain, axis=1, keepdims=True)
        high = square.astype(BF16).astype(F32)
        lane = lax.broadcasted_iota(jnp.int32, (step, 128), 1)
        extra = jnp.where(lane == 0, high, jnp.where(lane == 1, square - high, 0.0))
        o_ref[b * step : (b + 1) * step, wide : wide + 128] = extra.astype(BF16)


def gate_up(side, arrived, order, weights, gain):
    slots = arrived.shape[0] // 8
    return pl.pallas_call(
        gate_up_kernel,
        out_shape=jax.ShapeDtypeStruct((slots, weights.shape[1] + 128), BF16),
        in_specs=[pl.BlockSpec(memory_space=pltpu.SMEM)] + [pl.BlockSpec(memory_space=pltpu.VMEM)] * 4,
        scratch_shapes=[pltpu.VMEM((slots, weights.shape[0]), BF16)],
        compiler_params=pltpu.CompilerParams(vmem_limit_bytes=48 << 20),
        name="gate_up",
    )(side, arrived, order, weights, gain[None, :])


def down_kernel(h_ref, order_ref, w_ref, o_ref, *, by_x):
    step = order_ref.shape[0]
    quarter = step // 4
    lanes = o_ref.shape[1]
    for a in range(h_ref.shape[0] // step):
        found = jnp.dot(
            h_ref[a * step : (a + 1) * step, :], w_ref[...], preferred_element_type=F32
        )
        for e in range(4):
            b = e // 2 * 8 + a * 2 + e % 2 if by_x else a * 4 + e
            piece = found[e * quarter : (e + 1) * quarter]
            piece = jnp.concatenate(
                [piece[:, c * lanes : (c + 1) * lanes] for c in range(4)], axis=0
            ).astype(BF16)
            o_ref[b * step : (b + 1) * step, :] = jnp.dot(
                order_ref[...], piece, preferred_element_type=F32
            ).astype(BF16)


def down(hidden, order, weights, by_x, name):
    lanes = weights.shape[1] // 4
    return pl.pallas_call(
        functools.partial(down_kernel, by_x=by_x),
        out_shape=jax.ShapeDtypeStruct((hidden.shape[0] * 4, lanes), BF16),
        compiler_params=pltpu.CompilerParams(vmem_limit_bytes=48 << 20),
        name=name,
    )(hidden, order, weights)


def combine_kernel(x_ref, order_ref, w_ref, state_ref, o_ref, rows_ref):
    step = order_ref.shape[0]
    quarter = step // 4
    lanes = x_ref.shape[1]
    for b in range(x_ref.shape[0] // step):
        moved = jnp.dot(
            order_ref[...], x_ref[b * step : (b + 1) * step, :], preferred_element_type=F32
        ).astype(BF16)
        for c in range(4):
            rows_ref[b * quarter : (b + 1) * quarter, c * lanes : (c + 1) * lanes] = moved[
                c * quarter : (c + 1) * quarter
            ]
    routed = lax.dot_general(
        w_ref[...], rows_ref[...], (((0,), (0,)), ((), ())), preferred_element_type=F32
    )
    tokens = state_ref.shape[0]
    o_ref[...] = (state_ref[...] + routed[:tokens] + routed[tokens:]).astype(BF16)


def combine(returned, order, weights, state):
    slots = weights.shape[0]
    return pl.pallas_call(
        combine_kernel,
        out_shape=jax.ShapeDtypeStruct(state.shape, BF16),
        scratch_shapes=[pltpu.VMEM((slots, state.shape[1]), BF16)],
        compiler_params=pltpu.CompilerParams(vmem_limit_bytes=48 << 20),
        name="combine",
    )(returned, order, weights, state)


def attend_kernel(place, q_ref, k_ref, v_ref, o_ref, *, heads, piece, tokens):
    step = 512
    keys, size = k_ref.shape
    blocks = keys // piece
    factor = math.log2(math.e) / math.sqrt(size)
    block = lax.broadcasted_iota(jnp.int32, (blocks, 1, step), 0)
    core = jnp.where(block >= blocks // 2, 1 - place[1], place[1])
    begin = (block % (blocks // 2) * 2 + core) * tokens + place[2] * piece - place[0]
    row = lax.broadcasted_iota(jnp.int32, (blocks, 1, step), 2) // heads
    inner = lax.broadcasted_iota(jnp.int32, (blocks, piece, step), 1)
    line = lax.broadcasted_iota(jnp.int32, (16, step), 0)
    for i in range(q_ref.shape[0] // step):
        scores = lax.dot_general(
            k_ref[...],
            q_ref[i * step : (i + 1) * step, :],
            (((1,), (1,)), ((), ())),
            preferred_element_type=F32,
        )
        ahead = row + i * step // heads - begin
        scores = (scores * factor).reshape(blocks, piece, step)
        masked = jnp.where(inner <= ahead, scores, -1e30).reshape(keys, step)
        best = jnp.max(masked, axis=0, keepdims=True)
        best = jnp.maximum(best, FLOOR).astype(BF16).astype(F32)
        prob = jnp.exp2(masked - best)
        total = jnp.sum(prob, axis=0, keepdims=True)
        high = total.astype(BF16).astype(F32)
        summed = move(v_ref[...], prob.astype(BF16))
        o_ref[0:size, i * step : (i + 1) * step] = summed.astype(BF16)
        extra = jnp.where(line == 1, high, jnp.where(line == 2, total - high, 0.0))
        extra = jnp.where(line == 0, best, extra)
        o_ref[size : size + 16, i * step : (i + 1) * step] = extra.astype(BF16)


def move(matrix, rows):
    return lax.dot_general(matrix, rows, (((0,), (0,)), ((), ())), preferred_element_type=F32)


def attend(place, rows, keys, values, heads, piece, tokens):
    count, size = rows.shape
    return pl.pallas_call(
        functools.partial(attend_kernel, heads=heads, piece=piece, tokens=tokens),
        out_shape=jax.ShapeDtypeStruct((size + 16, count), BF16),
        in_specs=[pl.BlockSpec(memory_space=pltpu.SMEM)] + [pl.BlockSpec(memory_space=pltpu.VMEM)] * 3,
        compiler_params=pltpu.CompilerParams(vmem_limit_bytes=48 << 20),
        name="attend",
    )(place, rows, keys, values)


def body(queries, keys, values, resid, gain, expert_ids, gate_scores, w_gate_up, w_down, w_out):
    tokens, heads, size = queries.shape
    y, zl, core = lax.axis_index("y"), lax.axis_index("zl"), lax.axis_index("core")
    zh, x = lax.axis_index("zh"), lax.axis_index("x")
    ctx_place = (y * 8 + zl) * 2 + core
    ctx_count = 64
    width = resid.shape[1]

    piece = tokens // 4
    pair = jnp.stack([keys, values], axis=0)
    pair = lax.dynamic_index_in_dim(pair, zh, 2, keepdims=False)
    pair = lax.dynamic_slice_in_dim(pair, x * piece, piece, 1)
    pair = jnp.broadcast_to(pair[None], (8,) + pair.shape)
    line = w_out.reshape(-1, D)
    line = jnp.concatenate([line, partner(line, "zl", 4)], axis=0)
    pair = first = lax.all_to_all(pair, "zl", 0, 0, tiled=True)
    rows = queries.reshape(tokens * heads, size)
    beside = partner(rows, "x", 2)
    pair = after(pair, beside)
    pair = jnp.broadcast_to(pair[None], (4,) + pair.shape)
    pair = second = lax.all_to_all(pair, "y", 0, 0, tiled=True)
    across = partner(jnp.concatenate([beside, after(rows, first)], axis=0), "x", 1)
    line = double(line, 2, first)
    found = partner(line, "zl", 1)
    line = jnp.concatenate([after(line, second), found], axis=0)
    pair = after(pair, across)
    pair = jnp.stack([pair, shift(pair, "core", 1)], axis=0)
    all_keys = pair[:, :, :, 0].reshape(-1, size)
    all_values = pair[:, :, :, 1].reshape(-1, size)

    place = jnp.stack([ctx_place * tokens, core, x]).astype(jnp.int32)
    line = after(line, all_keys)
    line = jnp.broadcast_to(line[None], (4,) + line.shape)
    near = lax.all_to_all(line, "y", 0, 0, tiled=True).reshape(-1, D)
    parts, found = [], place
    asked = [(2, beside), (3, across[: tokens * heads]), (1, across[tokens * heads :])]
    for bit, theirs in asked:
        theirs = after(theirs, found)
        found = attend(place, theirs, all_keys, all_values, heads, piece, tokens)
        parts.append(partner(found, "x", bit))
    rows = after(rows, found)
    parts.append(attend(place, rows, all_keys, all_values, heads, piece, tokens))
    near = after(near, parts)
    far = shift(near, "core", 1)

    bests = [part[size].astype(F32) for part in parts]
    best = functools.reduce(jnp.maximum, bests)
    above = jnp.zeros((size, tokens * heads), F32)
    below = jnp.zeros((tokens * heads,), F32)
    for part, top in zip(parts, bests):
        scale = jnp.exp2(top - best)
        above = above + part[:size].astype(F32) * scale[None, :]
        below = below + (part[size + 1].astype(F32) + part[size + 2].astype(F32)) * scale
    context = (above / below[None, :]).astype(BF16).T.reshape(tokens, heads, size)

    order = feature_order(zl, core, heads, size)
    ordered = jnp.dot(
        context.reshape(tokens, heads * size), order, preferred_element_type=F32
    ).astype(BF16)
    mine = jnp.stack([zh]).astype(jnp.int32)
    half = sum_along_x(project(1 - mine, ordered, near, far)).astype(BF16)
    own = after(project(mine, ordered, near, far), half)
    attended = sum_along_x(own) + shift(half, "zh", 1).astype(F32)
    state = resid.astype(F32) + attended
    scaled = (state * gain[None, :]).astype(BF16)

    slots = ctx_count * MOST
    ids = after(expert_ids, ordered).T
    expert = jnp.arange(ctx_count, dtype=jnp.int32)
    named = (ids[:, None, :] == expert[None, :, None]).astype(F32)
    weight = (gate_scores / jnp.sum(gate_scores, axis=1, keepdims=True)).T
    weight = jnp.sum(named * weight[:, None, :], axis=0)
    named = jnp.sum(named, axis=0).astype(BF16)
    token = jnp.arange(tokens, dtype=jnp.int32)
    before = (token[:, None] < token[None, :]).astype(BF16)
    rank = jnp.dot(named, before, preferred_element_type=F32)
    line = jnp.arange(slots, dtype=jnp.int32)
    spread = (line[:, None] // MOST == expert[None, :]).astype(BF16)
    weight_high = weight.astype(BF16)
    weight_low = (weight - weight_high.astype(F32)).astype(BF16)
    rank = jnp.where(named > 0, rank, -1.0).astype(BF16)
    tables = jnp.concatenate([rank, weight_high, weight_low], axis=1)
    tables = jnp.dot(spread, tables, preferred_element_type=F32)
    live = tables[:, :tokens] == (line % MOST).astype(F32)[:, None]
    mixing = jnp.where(jnp.concatenate([live, live], axis=1), tables[:, tokens:], 0.0).astype(BF16)

    lanes = width // 4
    order = swap_order()
    outgoing = down(live.astype(BF16), order, scaled, False, "dispatch")
    outgoing = outgoing.reshape(ctx_count, 4 * MOST, lanes)
    arrived = lax.all_to_all(outgoing, CTX, 0, 0, tiled=True).reshape(4 * slots, lanes)

    units = w_gate_up.shape[3]
    weights = w_gate_up.reshape(width, 2 * units)
    shape = (4, slots // 8, 2 * units + 128)
    half = sum_along_x(gate_up(1 - mine, arrived, order, weights, gain).reshape(shape)).astype(BF16)
    own = after(gate_up(mine, arrived, order, weights, gain).reshape(shape), half)
    part = sum_along_x(own) + shift(half, "zh", 1).astype(F32)
    square = part[:, 2 * units : 2 * units + 1] + part[:, 2 * units + 1 : 2 * units + 2]
    inverse = lax.rsqrt(square / D + EPSILON)
    hidden = (jax.nn.silu(part[:, :units] * inverse) * (part[:, units : 2 * units] * inverse)).astype(
        BF16
    )
    other = shift(hidden, "zh", 1)
    hidden = jnp.where(
        zh == 0, jnp.stack([hidden, other], axis=0), jnp.stack([other, hidden], axis=0)
    )
    hidden = lax.all_gather(hidden, "x", axis=0).reshape(slots, units)
    result = down(hidden, order, w_down[0], True, "down").reshape(ctx_count, 4 * MOST, lanes)
    returned = lax.all_to_all(result, CTX, 0, 0, tiled=True).reshape(4 * slots, lanes)
    mixed = combine(returned, order, mixing, state)
    return (context, mixed)


def solution(mesh):
    mesh = Mesh(mesh.devices.reshape(4, 8, 2, 2, 4), CTX + EXP)
    in_specs = (
        P(CTX, EXP, None),
        P(CTX, None, None),
        P(CTX, None, None),
        P(CTX, EXP),
        P(EXP),
        P(CTX, None),
        P(CTX, None),
        P(CTX, EXP, None, None),
        P(CTX, None, EXP),
        P(EXP, CTX, None),
    )
    out_specs = (P(CTX, EXP, None), P(CTX, EXP))
    return jax.shard_map(body, mesh=mesh, in_specs=in_specs, out_specs=out_specs, check_vma=False)
```

```python
import functools
import math

import jax
import jax.numpy as jnp
from jax import lax
from jax.experimental import pallas as pl
from jax.experimental.pallas import tpu as pltpu
from jax.sharding import Mesh, PartitionSpec as P

D = 4096
KVH = 2
TOPK = 8
MOST = 10
FLOOR = -1e20
EPSILON = 1e-06
CTX = ("y", "zl", "core")
EXP = ("zh", "x")
SIZES = {"y": 4, "zl": 8, "core": 2, "zh": 2, "x": 4}
F32 = jnp.float32
BF16 = jnp.bfloat16


def shift(value, axis, step):
    count = SIZES[axis]
    return lax.ppermute(value, axis, [(i, (i + step) % count) for i in range(count)])


def partner(value, axis, bit):
    return lax.ppermute(value, axis, [(i, i ^ bit) for i in range(SIZES[axis])])


def after(value, earlier):
    return lax.optimization_barrier((value, earlier))[0]


def double(rows, bit, earlier):
    rows = after(rows, earlier)
    return jnp.concatenate([rows, partner(rows, "zl", bit)], axis=0)


def feature_order(zl, core, heads, size):
    place = lax.broadcasted_iota(jnp.int32, (heads * size, heads * size), 1)
    source = lax.broadcasted_iota(jnp.int32, (heads * size, heads * size), 0)
    inner = place % (2 * heads)
    slot = place // (2 * heads)
    bits = slot % 8
    from_zl = zl ^ (bits // 4 + bits // 2 % 2 * 2 + bits % 2 * 4)
    from_core = jnp.where(slot >= 32, 1 - core, core)
    block = (slot // 8 % 4 * 8 + from_zl) * 2 + from_core
    return (source == inner // 2 * size + block * 2 + inner % 2).astype(BF16)


def project_kernel(side, c_ref, near_ref, far_ref, o_ref):
    half = near_ref.shape[0]
    width = o_ref.shape[2]
    part = jnp.dot(c_ref[:, :half], near_ref[...], preferred_element_type=F32)
    part = part + jnp.dot(c_ref[:, half:], far_ref[...], preferred_element_type=F32)
    for i in range(o_ref.shape[0]):
        o_ref[i] = part[:, i * width : (i + 1) * width].astype(BF16)


def project(side, ordered, near, far):
    tokens = ordered.shape[0]
    width = D // 8
    return pl.pallas_call(
        project_kernel,
        out_shape=jax.ShapeDtypeStruct((4, tokens, width), BF16),
        grid_spec=pltpu.PrefetchScalarGridSpec(
            num_scalar_prefetch=1,
            grid=(2,),
            in_specs=[
                pl.BlockSpec(ordered.shape, lambda i, side: (0, 0)),
                pl.BlockSpec((near.shape[0], 2 * width), lambda i, side: (0, side[0] * 2 + i)),
                pl.BlockSpec((near.shape[0], 2 * width), lambda i, side: (0, side[0] * 2 + i)),
            ],
            out_specs=pl.BlockSpec((2, tokens, width), lambda i, side: (i, 0, 0)),
        ),
        compiler_params=pltpu.CompilerParams(vmem_limit_bytes=32 << 20),
        name="project",
    )(side, ordered, near, far)


def sum_along_x(parts):
    return jnp.sum(lax.all_to_all(parts, "x", 0, 0, tiled=True).astype(F32), axis=0)


def swap_order():
    count = 16 * MOST
    into = lax.broadcasted_iota(jnp.int32, (count, count), 0)
    source = lax.broadcasted_iota(jnp.int32, (count, count), 1)
    outer, inner, rank = into // (4 * MOST), into // MOST % 4, into % MOST
    return (source == (inner * 4 + outer) * MOST + rank).astype(BF16)


def gate_up_kernel(side, x_ref, order_ref, w_ref, gain_ref, o_ref, rows_ref):
    step = order_ref.shape[0]
    begin = pl.multiple_of(side[0] * (x_ref.shape[0] // 2), 16)
    quarter = step // 4
    lanes = x_ref.shape[1]
    for b in range(0, x_ref.shape[0] // step // 2, 2):
        first = x_ref[pl.ds(begin + b * step, step), :]
        second = x_ref[pl.ds(begin + (b + 1) * step, step), :]
        moved = jnp.dot(
            order_ref[...],
            jnp.concatenate([first, second], axis=1),
            preferred_element_type=F32,
        ).astype(BF16)
        for k in range(2):
            for c in range(4):
                rows_ref[
                    (b + k) * quarter : (b + k + 1) * quarter, c * lanes : (c + 1) * lanes
                ] = moved[c * quarter : (c + 1) * quarter, k * lanes : (k + 1) * lanes]
    wide = w_ref.shape[1]
    inverse = 1.0 / gain_ref[...]
    step = rows_ref.shape[0]
    for b in range(rows_ref.shape[0] // step):
        rows = rows_ref[b * step : (b + 1) * step, :]
        part = jnp.dot(rows, w_ref[...], preferred_element_type=F32)
        o_ref[b * step : (b + 1) * step, 0:wide] = part.astype(BF16)
        plain = rows.astype(F32) * inverse
        square = jnp.sum(plain * plain, axis=1, keepdims=True)
        high = square.astype(BF16).astype(F32)
        lane = lax.broadcasted_iota(jnp.int32, (step, 128), 1)
        extra = jnp.where(lane == 0, high, jnp.where(lane == 1, square - high, 0.0))
        o_ref[b * step : (b + 1) * step, wide : wide + 128] = extra.astype(BF16)


def gate_up(side, arrived, order, weights, gain):
    slots = arrived.shape[0] // 8
    return pl.pallas_call(
        gate_up_kernel,
        out_shape=jax.ShapeDtypeStruct((slots, weights.shape[1] + 128), BF16),
        in_specs=[pl.BlockSpec(memory_space=pltpu.SMEM)] + [pl.BlockSpec(memory_space=pltpu.VMEM)] * 4,
        scratch_shapes=[pltpu.VMEM((slots, weights.shape[0]), BF16)],
        compiler_params=pltpu.CompilerParams(vmem_limit_bytes=48 << 20),
        name="gate_up",
    )(side, arrived, order, weights, gain[None, :])


def down_kernel(h_ref, order_ref, w_ref, o_ref, *, by_x):
    step = order_ref.shape[0]
    quarter = step // 4
    lanes = o_ref.shape[1]
    found = jnp.dot(h_ref[...], w_ref[...], preferred_element_type=F32)
    for a in range(h_ref.shape[0] // step):
        for e in range(0, 4, 2):
            b = e // 2 * 8 + a * 2 if by_x else a * 4 + e
            begin = a * step + e * quarter
            pieces = [
                jnp.concatenate(
                    [
                        found[begin + k * quarter : begin + (k + 1) * quarter, c * lanes : (c + 1) * lanes]
                        for c in range(4)
                    ],
                    axis=0,
                )
                for k in range(2)
            ]
            moved = jnp.dot(
                order_ref[...],
                jnp.concatenate(pieces, axis=1).astype(BF16),
                preferred_element_type=F32,
            ).astype(BF16)
            o_ref[b * step : (b + 1) * step, :] = moved[:, :lanes]
            o_ref[(b + 1) * step : (b + 2) * step, :] = moved[:, lanes:]


def down(hidden, order, weights, by_x, name):
    lanes = weights.shape[1] // 4
    return pl.pallas_call(
        functools.partial(down_kernel, by_x=by_x),
        out_shape=jax.ShapeDtypeStruct((hidden.shape[0] * 4, lanes), BF16),
        compiler_params=pltpu.CompilerParams(vmem_limit_bytes=48 << 20),
        name=name,
    )(hidden, order, weights)


def combine_kernel(x_ref, order_ref, w_ref, state_ref, o_ref, rows_ref):
    step = order_ref.shape[0]
    quarter = step // 4
    lanes = x_ref.shape[1]
    for b in range(x_ref.shape[0] // step):
        moved = jnp.dot(
            order_ref[...], x_ref[b * step : (b + 1) * step, :], preferred_element_type=F32
        ).astype(BF16)
        for c in range(4):
            rows_ref[b * quarter : (b + 1) * quarter, c * lanes : (c + 1) * lanes] = moved[
                c * quarter : (c + 1) * quarter
            ]
    routed = lax.dot_general(
        w_ref[...], rows_ref[...], (((0,), (0,)), ((), ())), preferred_element_type=F32
    )
    tokens = state_ref.shape[0]
    o_ref[...] = (state_ref[...] + routed[:tokens] + routed[tokens:]).astype(BF16)


def combine(returned, order, weights, state):
    slots = weights.shape[0]
    return pl.pallas_call(
        combine_kernel,
        out_shape=jax.ShapeDtypeStruct(state.shape, BF16),
        scratch_shapes=[pltpu.VMEM((slots, state.shape[1]), BF16)],
        compiler_params=pltpu.CompilerParams(vmem_limit_bytes=48 << 20),
        name="combine",
    )(returned, order, weights, state)


def attend_kernel(place, q_ref, k_ref, v_ref, o_ref, *, heads, piece, tokens):
    step = 512
    keys, size = k_ref.shape
    blocks = keys // piece
    factor = math.log2(math.e) / math.sqrt(size)
    block = lax.broadcasted_iota(jnp.int32, (blocks, 1, step), 0)
    core = jnp.where(block >= blocks // 2, 1 - place[1], place[1])
    begin = (block % (blocks // 2) * 2 + core) * tokens + place[2] * piece - place[0]
    row = lax.broadcasted_iota(jnp.int32, (blocks, 1, step), 2) // heads
    inner = lax.broadcasted_iota(jnp.int32, (blocks, piece, step), 1)
    line = lax.broadcasted_iota(jnp.int32, (16, step), 0)
    for i in range(q_ref.shape[0] // step):
        scores = lax.dot_general(
            k_ref[...],
            q_ref[i * step : (i + 1) * step, :],
            (((1,), (1,)), ((), ())),
            preferred_element_type=F32,
        )
        ahead = row + i * step // heads - begin
        scores = (scores * factor).reshape(blocks, piece, step)
        masked = jnp.where(inner <= ahead, scores, -1e30).reshape(keys, step)
        best = jnp.max(masked, axis=0, keepdims=True)
        best = jnp.maximum(best, FLOOR).astype(BF16).astype(F32)
        prob = jnp.exp2(masked - best)
        total = jnp.sum(prob, axis=0, keepdims=True)
        high = total.astype(BF16).astype(F32)
        summed = move(v_ref[...], prob.astype(BF16))
        o_ref[0:size, i * step : (i + 1) * step] = summed.astype(BF16)
        extra = jnp.where(line == 1, high, jnp.where(line == 2, total - high, 0.0))
        extra = jnp.where(line == 0, best, extra)
        o_ref[size : size + 16, i * step : (i + 1) * step] = extra.astype(BF16)


def move(matrix, rows):
    return lax.dot_general(matrix, rows, (((0,), (0,)), ((), ())), preferred_element_type=F32)


def attend(place, rows, keys, values, heads, piece, tokens):
    count, size = rows.shape
    return pl.pallas_call(
        functools.partial(attend_kernel, heads=heads, piece=piece, tokens=tokens),
        out_shape=jax.ShapeDtypeStruct((size + 16, count), BF16),
        in_specs=[pl.BlockSpec(memory_space=pltpu.SMEM)] + [pl.BlockSpec(memory_space=pltpu.VMEM)] * 3,
        compiler_params=pltpu.CompilerParams(vmem_limit_bytes=48 << 20),
        name="attend",
    )(place, rows, keys, values)


def body(queries, keys, values, resid, gain, expert_ids, gate_scores, w_gate_up, w_down, w_out):
    tokens, heads, size = queries.shape
    y, zl, core = lax.axis_index("y"), lax.axis_index("zl"), lax.axis_index("core")
    zh, x = lax.axis_index("zh"), lax.axis_index("x")
    ctx_place = (y * 8 + zl) * 2 + core
    ctx_count = 64
    width = resid.shape[1]

    piece = tokens // 4
    pair = jnp.stack([keys, values], axis=0)
    pair = lax.dynamic_index_in_dim(pair, zh, 2, keepdims=False)
    pair = lax.dynamic_slice_in_dim(pair, x * piece, piece, 1)
    pair = jnp.broadcast_to(pair[None], (8,) + pair.shape)
    line = w_out.reshape(-1, D)
    line = jnp.concatenate([line, partner(line, "zl", 4)], axis=0)
    pair = first = lax.all_to_all(pair, "zl", 0, 0, tiled=True)
    rows = queries.reshape(tokens * heads, size)
    beside = partner(rows, "x", 2)
    pair = after(pair, beside)
    pair = jnp.broadcast_to(pair[None], (4,) + pair.shape)
    pair = second = lax.all_to_all(pair, "y", 0, 0, tiled=True)
    across = partner(jnp.concatenate([beside, after(rows, first)], axis=0), "x", 1)
    line = double(line, 2, first)
    found = partner(line, "zl", 1)
    line = jnp.concatenate([after(line, second), found], axis=0)
    pair = after(pair, across)
    pair = jnp.stack([pair, shift(pair, "core", 1)], axis=0)
    all_keys = pair[:, :, :, 0].reshape(-1, size)
    all_values = pair[:, :, :, 1].reshape(-1, size)

    place = jnp.stack([ctx_place * tokens, core, x]).astype(jnp.int32)
    line = after(line, all_keys)
    line = jnp.broadcast_to(line[None], (4,) + line.shape)
    near = lax.all_to_all(line, "y", 0, 0, tiled=True).reshape(-1, D)
    parts, found = [], place
    asked = [(2, beside), (3, across[: tokens * heads]), (1, across[tokens * heads :])]
    for bit, theirs in asked:
        theirs = after(theirs, found)
        found = attend(place, theirs, all_keys, all_values, heads, piece, tokens)
        parts.append(partner(found, "x", bit))
    rows = after(rows, found)
    parts.append(attend(place, rows, all_keys, all_values, heads, piece, tokens))
    near = after(near, parts)
    far = shift(near, "core", 1)

    bests = [part[size].astype(F32) for part in parts]
    best = functools.reduce(jnp.maximum, bests)
    above = jnp.zeros((size, tokens * heads), F32)
    below = jnp.zeros((tokens * heads,), F32)
    for part, top in zip(parts, bests):
        scale = jnp.exp2(top - best)
        above = above + part[:size].astype(F32) * scale[None, :]
        below = below + (part[size + 1].astype(F32) + part[size + 2].astype(F32)) * scale
    context = (above / below[None, :]).astype(BF16).T.reshape(tokens, heads, size)

    order = feature_order(after(zl, parts[3]), after(core, parts[3]), heads, size)
    ordered = jnp.dot(
        context.reshape(tokens, heads * size), order, preferred_element_type=F32
    ).astype(BF16)
    mine = jnp.stack([zh]).astype(jnp.int32)
    half = sum_along_x(project(1 - mine, ordered, near, far)).astype(BF16)
    own = after(project(mine, ordered, near, far), half)
    attended = sum_along_x(own) + shift(half, "zh", 1).astype(F32)
    state = resid.astype(F32) + attended
    scaled = (state * gain[None, :]).astype(BF16)

    slots = ctx_count * MOST
    ids = after(expert_ids, ordered).T
    expert = jnp.arange(ctx_count, dtype=jnp.int32)
    named = (ids[:, None, :] == expert[None, :, None]).astype(F32)
    weight = (gate_scores / jnp.sum(gate_scores, axis=1, keepdims=True)).T
    weight = jnp.sum(named * weight[:, None, :], axis=0)
    named = jnp.sum(named, axis=0).astype(BF16)
    token = jnp.arange(tokens, dtype=jnp.int32)
    before = (token[:, None] < token[None, :]).astype(BF16)
    rank = jnp.dot(named, before, preferred_element_type=F32)
    line = jnp.arange(slots, dtype=jnp.int32)
    spread = (line[:, None] // MOST == expert[None, :]).astype(BF16)
    weight_high = weight.astype(BF16)
    weight_low = (weight - weight_high.astype(F32)).astype(BF16)
    rank = jnp.where(named > 0, rank, -1.0).astype(BF16)
    tables = jnp.concatenate([rank, weight_high, weight_low], axis=1)
    tables = jnp.dot(spread, tables, preferred_element_type=F32)
    live = tables[:, :tokens] == (line % MOST).astype(F32)[:, None]
    mixing = jnp.where(jnp.concatenate([live, live], axis=1), tables[:, tokens:], 0.0).astype(BF16)

    lanes = width // 4
    order = swap_order()
    outgoing = down(live.astype(BF16), order, scaled, False, "dispatch")
    outgoing = outgoing.reshape(ctx_count, 4 * MOST, lanes)
    arrived = lax.all_to_all(outgoing, CTX, 0, 0, tiled=True).reshape(4 * slots, lanes)

    units = w_gate_up.shape[3]
    weights = w_gate_up.reshape(width, 2 * units)
    shape = (4, slots // 8, 2 * units + 128)
    half = sum_along_x(gate_up(1 - mine, arrived, order, weights, gain).reshape(shape)).astype(BF16)
    own = after(gate_up(mine, arrived, order, weights, gain).reshape(shape), half)
    part = sum_along_x(own) + shift(half, "zh", 1).astype(F32)
    square = part[:, 2 * units : 2 * units + 1] + part[:, 2 * units + 1 : 2 * units + 2]
    inverse = lax.rsqrt(square / D + EPSILON)
    hidden = (jax.nn.silu(part[:, :units] * inverse) * (part[:, units : 2 * units] * inverse)).astype(
        BF16
    )
    other = shift(hidden, "zh", 1)
    hidden = jnp.where(
        zh == 0, jnp.stack([hidden, other], axis=0), jnp.stack([other, hidden], axis=0)
    )
    hidden = lax.all_gather(hidden, "x", axis=0).reshape(slots, units)
    result = down(hidden, order, w_down[0], True, "down").reshape(ctx_count, 4 * MOST, lanes)
    returned = lax.all_to_all(result, CTX, 0, 0, tiled=True).reshape(4 * slots, lanes)
    mixed = combine(returned, order, mixing, state)
    return (context, mixed)


def solution(mesh):
    mesh = Mesh(mesh.devices.reshape(4, 8, 2, 2, 4), CTX + EXP)
    in_specs = (
        P(CTX, EXP, None),
        P(CTX, None, None),
        P(CTX, None, None),
        P(CTX, EXP),
        P(EXP),
        P(CTX, None),
        P(CTX, None),
        P(CTX, EXP, None, None),
        P(CTX, None, EXP),
        P(EXP, CTX, None),
    )
    out_specs = (P(CTX, EXP, None), P(CTX, EXP))
    return jax.shard_map(body, mesh=mesh, in_specs=in_specs, out_specs=out_specs, check_vma=False)
```
